128 devices in a mesh: row: 8 (over y, core), col: 16 (over x, z).
Axes of the slice: x: 4, y: 4, z: 4, core: 2. Of those that a mesh axis runs over, the one named last changes fastest.
Arguments:
- queries: bfloat16 [4, 16384, 256], P(None, ('row', 'col'))
- probes: int32 [4, 16384, 2], P(None, ('row', 'col')), may hold values from 0 to 127, all different within a row; in each aligned block of 128 rows (0 to 127, 128 to 255, ..., all dimensions but the last counted through in order) at most 4 rows name the same one
- keys: bfloat16 [128, 1024, 256], P(('row', 'col')), may hold values from -6 to 6
- values: bfloat16 [128, 1024, 256], P(('row', 'col')), may hold values from -6 to 6
- bucket_home: int32 [128], replicated, may hold values from 0 to 127, each once
- bucket_rows: int32 [128], replicated, may hold values from 1 to 1024, 49152 in all
Outputs:
- attended: bfloat16 [4, 16384, 256], P(None, ('row', 'col'))
The draws below stay inside these ranges and needn't reach their ends.
Inputs may be any that keep to these rules, and one draw needn't show every extreme that they name: `probes`: each request names two different buckets; among the requests of one device in one step no bucket is named more than 4 times, a bound that some block reaches. `bucket_home`: each device holds exactly one bucket. `bucket_rows`: some bucket fills all 8 blocks.
All inputs are finite; a program needn't handle non-finite values.
Results may differ from the reference program's by a relative error of at most 0.007.
Values may be sent and summed in bfloat16 or wider, within the bound.
No kernel may reach another device: no remote copies, remote signals or barrier semaphores. Data moves between devices by JAX's collectives and lax.ppermute only.
A program may use at most 64 MiB of HBM per device.

```python
import math
import jax
import jax.numpy as jnp
import numpy as np
from jax import lax

H = 8
HD = 32
D = 256
BLK = 128
SLOTS = 8
STEPS = 4
Q_DEV = 128
NB = 128
REQ = 16384
CAP = 4


def draw_queries(key, part):
    first_key = jax.random.fold_in(jax.random.fold_in(key, 11), 0)
    base = jax.random.normal(first_key, (STEPS, REQ, D), jnp.float32)
    return base.astype(jnp.bfloat16)


def level_of(own_key, extent, cuts, low, top_value):
    level, own = 1.0, jax.random.fold_in(own_key, 6)
    for dim, blocks in cuts:
        heights = jnp.exp(jax.random.uniform(jax.random.fold_in(own, dim), (blocks,), jnp.float32, low / len(cuts), top_value / len(cuts)))
        level = level * jnp.repeat(heights, extent[dim] // blocks).reshape([-1 if axis == dim else 1 for axis in range(len(extent))])
    return level


def split_up(count, total, bound, lean):
    portions = [(1 << 20) // math.isqrt(rank ** lean) + 1 for rank in range(2, count + 1)]
    surplus, holding = total - bound - (count - 1), [1] * (count - 1)
    while surplus > 0:
        free = [i for i in range(count - 1) if holding[i] < bound]
        mass, remaining = sum([portions[i] for i in free]), surplus
        for i in free:
            addition = min(bound - holding[i], max(1, remaining * portions[i] // mass), surplus)
            holding[i] = holding[i] + addition
            surplus = surplus - addition
    return np.array([bound] + holding)


def ragged_sizes(stream_key, amount, total, most, lean):
    if amount == 2:
        one = jax.random.randint(stream_key, (), max(1, total - most), min(most, total - 1) + 1)
        return jnp.stack([one, total - one])
    lengths = jnp.asarray(split_up(amount, total, most, lean), jnp.int32)
    couples = (amount - 1) // 2
    giver, sink = lengths[1:1 + 2 * couples:2], lengths[2:2 + 2 * couples:2]
    slack = jnp.minimum(giver - 1, most - sink)
    moved = jax.random.randint(jax.random.fold_in(stream_key, 1), (couples,), 0, 1 << 20) % (slack + 1)
    lengths = lengths.at[1:1 + 2 * couples:2].set(giver - moved).at[2:2 + 2 * couples:2].set(sink + moved)
    return lengths[jax.random.permutation(jax.random.fold_in(stream_key, 2), amount)]


def shared_out(own_key, own, number, rows, count, top, limit, lean):
    ranking = jax.random.permutation(own_key, count)
    crowded, usual = load_shares(count, rows * top, limit, lean, True), load_shares(count, rows * top, limit, lean, False)
    places = jnp.arange(count)

    def named(lengths, offset_by):
        used = int((lengths > 0).sum())
        fixed = max(1, used // 4)
        passed = fixed + (places - fixed + offset_by * (used - fixed)) % max(1, count - fixed)
        return jnp.zeros((count,), jnp.int32).at[ranking[jnp.where(places < fixed, places, passed)]].set(jnp.asarray(lengths, jnp.int32))

    lengths = jnp.where(number % 4 == 0, named(crowded, number // 4), named(usual, number - number // 4 - 1))
    mixed = jax.random.permutation(jax.random.fold_in(own, 3), count)
    source_of, receiver = mixed[0:count // 2 * 2:2], mixed[1:count // 2 * 2:2]
    margin = jnp.minimum(lengths[source_of] - 1, limit - lengths[receiver]) // 2
    margin = jnp.where((source_of == ranking[0]) | (receiver == ranking[0]) | (lengths[receiver] == 0), 0, jnp.maximum(margin, 0))
    passed = jax.random.randint(jax.random.fold_in(own, 4), (count // 2,), 0, 1 << 20) % (margin + 1)
    lengths = lengths.at[source_of].add(-passed).at[receiver].add(passed)
    labels = jnp.searchsorted(jnp.cumsum(lengths), jnp.arange(rows * top), side="right").astype(jnp.int32)
    table = labels.reshape(top, rows).T
    table = table[jax.random.permutation(jax.random.fold_in(own, 1), rows)]
    offset_by = jax.random.randint(jax.random.fold_in(own, 2), (rows, 1), 0, top)
    return jnp.take_along_axis(table, (jnp.arange(top)[None, :] + offset_by) % top, axis=1)


def load_shares(amount, total, most, slope, full):
    portions = [(1 << 20) // math.isqrt(rank ** slope) + 1 for rank in range(1, amount + 1)]
    largest = most if full else min(most, max(-(-total // amount), total * portions[0] // sum(portions)))
    least = 1 if total - largest >= amount - 1 else 0
    holding, spare = [largest] + [least] * (amount - 1), total - largest - least * (amount - 1)
    while spare > 0:
        movable = [i for i in range(1, amount) if holding[i] < largest] or [i for i in range(1, amount) if holding[i] < most]
        whole, left = sum([portions[i] for i in movable]), spare
        for i in movable:
            extra = min(most - holding[i], max(1, left * portions[i] // whole), spare)
            holding[i] = holding[i] + extra
            spare = spare - extra
    return np.array(holding)


def gaussian(key, dims, scale, most, shards=(), kind=jnp.bfloat16):
    result = scale * jax.random.normal(key, dims, jnp.float32)
    if shards:
        result = result * level_of(key, dims, shards, -0.22, 0.18)
    return jnp.clip(result, -most, most).astype(kind)


def setup_inputs(seed: int = 0) -> dict:
    seeds = jax.random.split(jax.random.key(seed), 7)
    queries = draw_queries(jax.random.fold_in(seeds[6], 71), 0)
    probes_keys = jax.random.split(jax.random.fold_in(seeds[1], 1), STEPS * REQ // Q_DEV)
    probes_turns = jax.random.permutation(jax.random.fold_in(seeds[1], 3), STEPS * REQ // Q_DEV)
    probes = jax.vmap(lambda own, number: shared_out(jax.random.fold_in(seeds[1], 2), own, number, Q_DEV, NB, 2, CAP, 2))(probes_keys, probes_turns).reshape((STEPS, REQ, 2))
    keys = gaussian(seeds[2], (NB, SLOTS * BLK, D), 1.0, 6.0, ((0, 128),))
    values = gaussian(seeds[3], (NB, SLOTS * BLK, D), 1.0, 6.0, ((0, 128),))
    bucket_home = jax.random.permutation(seeds[4], NB).astype(jnp.int32)
    bucket_rows = ragged_sizes(seeds[5], NB, NB * SLOTS * BLK * 3 // 8, SLOTS * BLK, 2).astype(jnp.int32)
    return {"queries": queries, "probes": probes, "keys": keys, "values": values, "bucket_home": bucket_home, "bucket_rows": bucket_rows}


def reference(queries, probes, keys, values, bucket_home, bucket_rows):
    score_scale = 1.0 / math.sqrt(HD)
    total_rows = SLOTS * BLK
    group_size = math.gcd(STEPS * REQ, 64)
    groups = STEPS * REQ // group_size
    query_groups = queries.reshape(groups, group_size, D)
    probe_groups = probes.reshape(groups, group_size, 2)

    def one_group(pieces):
        query_block, probe_block = pieces
        device_ids = bucket_home[probe_block]
        key_rows = keys[device_ids].astype(jnp.float32).reshape(group_size, 2 * total_rows, H, HD)
        value_rows = values[device_ids].astype(jnp.float32).reshape(group_size, 2 * total_rows, H, HD)
        limits = bucket_rows[probe_block]
        valid_rows = (jnp.arange(total_rows, dtype=jnp.int32)[None, None, :] < limits[:, :, None]).reshape(group_size, 2 * total_rows)
        query_heads = query_block.astype(jnp.float32).reshape(group_size, H, HD)
        scores = jnp.einsum('bhd,bkhd->bhk', query_heads, key_rows) * score_scale
        scores = jnp.where(valid_rows[:, None, :], scores, -jnp.inf)
        highest = lax.optimization_barrier(jnp.max(scores, axis=-1, keepdims=True))
        weights = jnp.exp(scores - highest)
        total = lax.optimization_barrier(jnp.sum(weights, axis=-1))
        rounded = lax.optimization_barrier(weights.astype(jnp.bfloat16)).astype(jnp.float32)
        mixed = jnp.einsum('bhk,bkhd->bhd', rounded, value_rows) / total[:, :, None]
        return mixed.reshape(group_size, D).astype(jnp.bfloat16)
    attended = lax.map(one_group, (query_groups, probe_groups))
    return attended.reshape(STEPS, REQ, D)
```

```python
import math

import jax
import jax.numpy as jnp
from jax import lax
from jax.experimental import pallas as pl
from jax.experimental.pallas import tpu as pltpu
from jax.sharding import Mesh, PartitionSpec as P

H = 8
HD = 32
D = 256
KB = 256
QB = 256
CAP = 16
RET = 40
SCALE2 = math.log2(math.e) / math.sqrt(HD)
SAFE = 100.0
KEY_NORM2 = HD * 36.0
Q_LIMIT = (SAFE / SCALE2) ** 2 / KEY_NORM2 / 1.05

f32 = jnp.float32
bf16 = jnp.bfloat16
i32 = jnp.int32


def iota(shape, dim):
    return lax.broadcasted_iota(i32, shape, dim)


def dot(a, b):
    return jnp.dot(a, b, preferred_element_type=f32)


def dot_t(a, b):
    return lax.dot_general(a, b, (((1,), (1,)), ((), ())), preferred_element_type=f32)


def ones_where(cond):
    return jnp.where(cond, 1.0, 0.0).astype(bf16)


def dispatch_kernel(probes_ref, home_ref, q_ref, send_ref, pos_ref):
    steps = probes_ref.shape[0]
    n = 128
    eye = iota((n, n), 0) == iota((n, n), 1)
    home_row = jnp.broadcast_to(home_ref[...].astype(f32), (n, n))
    home = dot(jnp.where(eye, home_row, 0.0).astype(bf16), jnp.ones((n, n), bf16)).astype(i32)
    core = (home >> 4) & 1
    chip = ((home >> 5) << 4) + (home & 15)
    base = (chip * (2 * CAP) + core * CAP).astype(f32)
    tri = jnp.concatenate(
        [ones_where(iota((n, n), 0) < iota((n, n), 1)), jnp.ones((n, n), bf16)], axis=1
    )
    bucket = iota((n, n), 0)
    pos_rows = []
    for t in range(steps):
        for j in range(2):
            probe = probes_ref[t, j : j + 1, :]
            hit = bucket == probe
            counts = dot(ones_where(hit), tri)
            pos_rows.append(
                jnp.sum(jnp.where(hit, counts[:, :n] + base, 0.0), axis=0, keepdims=True)
            )
            base = base + counts[:, n:]
    pos = jnp.concatenate(pos_rows, axis=0).astype(i32)
    pos_ref[...] = pos
    rows = 512
    for block in range(send_ref.shape[0] // rows):
        where = iota((rows, n), 0) + block * rows
        pick = [
            ones_where((where == pos[2 * t : 2 * t + 1, :]) | (where == pos[2 * t + 1 : 2 * t + 2, :]))
            for t in range(steps)
        ]
        total = dot(pick[0], q_ref[0])
        for t in range(1, steps):
            total = total + dot(pick[t], q_ref[t])
        send_ref[block * rows : (block + 1) * rows, :] = total.astype(bf16)


def prepare_kernel(info_ref, k_own, v_own, k_other, v_other, kt_ref, vbd_ref, mean_ref):
    lane = iota((KB, 128), 1)
    for u in range(2):
        key_ref = (k_own, k_other)[u]
        value_ref = (v_own, v_other)[u]
        count = info_ref[1 + u]
        total = jnp.zeros((8, D), f32)
        for kb in range(1024 // KB):
            kt_ref[u, kb] = key_ref[kb * KB : (kb + 1) * KB, :].T
            valid = (iota((KB, D), 0) + kb * KB) < count
            value = jnp.where(valid, value_ref[kb * KB : (kb + 1) * KB, :], 0.0).astype(bf16)
            total = total + dot(jnp.ones((8, KB), bf16), value)
            ones = ones_where(valid[:, :128])
            for g in range(2):
                for hh in range(4):
                    mine = (lane >= hh * HD) & (lane < (hh + 1) * HD)
                    part = value[:, g * 128 : (g + 1) * 128]
                    vbd_ref[u, g, kb, hh * KB : (hh + 1) * KB, :128] = jnp.where(mine, part, 0.0).astype(bf16)
                    vbd_ref[u, g, kb, hh * KB : (hh + 1) * KB, 128:] = jnp.where(mine, ones, 0.0).astype(bf16)
        mean_ref[u] = total / count.astype(f32)


def split3(x):
    high = x.astype(bf16)
    rest = x - high.astype(f32)
    mid = rest.astype(bf16)
    low = (rest - mid.astype(f32)).astype(bf16)
    return high, mid, low


def mass_lanes(x):
    lane_in = iota((D, 128), 0)
    lane_out = iota((D, 128), 1)
    total = None
    for k, part in enumerate(split3(x)):
        pick = ones_where((lane_in == (lane_out - 8 * k) * HD) & (lane_out >= 8 * k) & (lane_out < 8 * k + 8))
        one = dot(part, pick)
        total = one if total is None else total + one
    return total.astype(bf16)


def attention_kernel(
    info_ref, recv_ref, kt_ref, vbd_ref, mean_ref, ret_ref,
    qc_ref, oc_ref, wc_ref, gt_ref, nz_ref, qm_ref, acc_ref, max_ref,
):
    n = 128
    groups = recv_ref.shape[0] // 8
    core = info_ref[0]
    qc_ref[...] = jnp.zeros(qc_ref.shape, bf16)
    oc_ref[...] = jnp.zeros(oc_ref.shape, bf16)
    wc_ref[...] = jnp.zeros(wc_ref.shape, bf16)
    upper = ones_where(iota((n, n), 0) < iota((n, n), 1))
    lower = ones_where(iota((n, n), 0) > iota((n, n), 1))
    head_sum = ones_where((iota((D, n), 0) // HD) == iota((D, n), 1))
    row_id = iota((n, n), 0)
    lane_id = iota((n, n), 1)

    offsets = []
    ends = []
    largest = jnp.zeros((n, n), f32)
    for j in range(2):
        packed = []
        for g in range(groups):
            q = recv_ref[8 * g : 8 * g + 8, j * CAP : (j + 1) * CAP, :].reshape(n, D)
            qf = q.astype(f32)
            used = ones_where(qf != 0.0)
            count = dot_t(jnp.ones((16, D), bf16), used)
            live = ones_where(count > 0.5)
            rank = dot(live, upper)
            size = jnp.sum(live[0:1, :].astype(f32)).astype(i32)
            gather = ones_where((rank[0:1, :].astype(i32) == row_id) & (count[0:1, :] > 0.5))
            packed.append((size, dot(gather, q).astype(bf16)))
            live_t = dot(used, jnp.ones((D, n), bf16)) > 0.5
            rank_t = dot(lower, ones_where(live_t)).astype(i32)
            gt_ref[j, g] = ones_where((rank_t == lane_id) & live_t)
            nz_ref[j, g] = ones_where(live_t)
            largest = jnp.maximum(largest, dot((qf * qf).astype(bf16), head_sum))
        offset = jnp.int32(0)
        mine = []
        for size, rows in packed:
            mine.append(offset)
            qc_ref[j, pl.ds(pl.multiple_of(offset, 16), n), :] = rows
            offset = offset + ((size + 15) >> 4) * 16
        offsets.append(mine)
        ends.append(offset)
    fast = jnp.max(largest) <= Q_LIMIT

    lane = iota((QB, 128), 1)

    def per_bucket(j, carry):
        u = j ^ core
        keys = info_ref[1 + u]
        blocks = (keys + KB - 1) // KB
        chunks = (jnp.where(j == 0, ends[0], ends[1]) + QB - 1) // QB

        def per_chunk(ch, carry):
            start = pl.multiple_of(ch * QB, QB)
            q = qc_ref[j, pl.ds(start, QB), :]
            for h in range(H):
                g, hh = h // 4, h % 4
                mine = (lane >= hh * HD) & (lane < (hh + 1) * HD)
                qm_ref[h] = jnp.where(mine, q[:, g * 128 : (g + 1) * 128], 0.0).astype(bf16)
            acc_ref[...] = jnp.zeros(acc_ref.shape, f32)

            @pl.when(fast)
            def _():
                max_ref[...] = jnp.zeros(max_ref.shape, f32)

                def block(kb, carry):
                    for g in range(2):
                        kt = kt_ref[u, kb, g * 128 : (g + 1) * 128, :]
                        total = acc_ref[g]
                        for hh in range(4):
                            s = dot(qm_ref[4 * g + hh], kt)
                            p = jnp.exp2(s * SCALE2).astype(bf16)
                            total = total + dot(p, vbd_ref[u, g, kb, hh * KB : (hh + 1) * KB, :])
                        acc_ref[g] = total
                    return carry

                lax.fori_loop(0, blocks, block, 0)

            @pl.when(jnp.logical_not(fast))
            def _():
                max_ref[...] = jnp.full(max_ref.shape, -3e38, f32)

                def scores(h, kb):
                    g = h // 4
                    s = dot(qm_ref[h], kt_ref[u, kb, g * 128 : (g + 1) * 128, :]) * SCALE2
                    return s, (iota((QB, KB), 1) + kb * KB) < keys

                def find(kb, carry):
                    for h in range(H):
                        g, hh = h // 4, h % 4
                        mine = (lane >= hh * HD) & (lane < (hh + 1) * HD)
                        s, valid = scores(h, kb)
                        top = jnp.max(jnp.where(valid, s, -3e38), axis=1, keepdims=True)
                        max_ref[g] = jnp.where(mine, jnp.maximum(max_ref[g], top), max_ref[g])
                    return carry

                lax.fori_loop(0, blocks, find, 0)

                def block(kb, carry):
                    for h in range(H):
                        g, hh = h // 4, h % 4
                        mine = (lane >= hh * HD) & (lane < (hh + 1) * HD)
                        s, valid = scores(h, kb)
                        top = jnp.max(jnp.where(mine, max_ref[g], -3e38), axis=1, keepdims=True)
                        p = jnp.where(valid, jnp.exp2(s - top), 0.0).astype(bf16)
                        acc_ref[g] += dot(p, vbd_ref[u, g, kb, hh * KB : (hh + 1) * KB, :])
                    return carry

                lax.fori_loop(0, blocks, block, 0)

            masses = []
            for g in range(2):
                acc = acc_ref[g]
                total = acc[:, 128:]
                oc_ref[j, pl.ds(start, QB), g * 128 : (g + 1) * 128] = (acc[:, :128] / total).astype(bf16)
                masses.append(jnp.log2(total) + max_ref[g])
            wc_ref[j, pl.ds(start, QB), :] = mass_lanes(jnp.concatenate(masses, axis=1))
            return carry

        return lax.fori_loop(0, chunks, per_chunk, carry)

    lax.fori_loop(0, 2, per_bucket, 0)

    spread = ones_where((iota((n, D), 1) % 32) == iota((n, D), 0))
    own_lanes = (iota((n, D), 1) // 32) == (iota((n, D), 0) % 8)
    means = []
    mean_masses = []
    for j in range(2):
        u = j ^ core
        means.append(mean_ref[u][0:1, :])
        log_rows = jnp.log2(jnp.full((8, D), info_ref[1 + u].astype(f32), f32))
        mean_masses.append(mass_lanes(log_rows)[0:1, :].astype(f32))
    for g in range(groups):
        mass_rows = jnp.zeros((64, D), f32)
        for j in range(2):
            start = pl.multiple_of(offsets[j][g], 16)
            gt = gt_ref[j, g]
            live = nz_ref[j, g].astype(f32) > 0.5
            live2 = jnp.concatenate([live, live], axis=1)
            rows = dot(gt, oc_ref[j, pl.ds(start, n), :])
            rows = jnp.where(live2, rows, means[j]).astype(bf16)
            ret_ref[8 * g : 8 * g + 8, j * CAP : (j + 1) * CAP, :] = rows.reshape(8, CAP, D)
            mass = dot(gt, wc_ref[j, pl.ds(start, n), :])
            mass = jnp.where(live, mass, mean_masses[j]).astype(bf16)
            wide = jnp.where(own_lanes, dot(mass, spread), 0.0).astype(bf16)
            out_row = iota((64, n), 0)
            slot = iota((64, n), 1)
            pick = ones_where((out_row == (slot // 16) * 8 + 2 * j + (slot % 16) // 8))
            mass_rows = mass_rows + dot(pick, wide)
        ret_ref[8 * g : 8 * g + 8, 32:40, :] = mass_rows.astype(bf16).reshape(8, 8, D)


def combine_kernel(pos_ref, ret_ref, out_ref):
    n = 128
    pos = pos_ref[...].astype(f32).T.astype(i32)
    all_rows = ret_ref[...].reshape(ret_ref.shape[0] * RET, D)
    mass_rows = ret_ref[:, 32:40, :].reshape(ret_ref.shape[0] * 8, D)
    lane_in = iota((D, D), 0) % 32
    widen = ones_where((lane_in < 24) & ((lane_in % 8) == (iota((D, D), 1) // HD)))
    lane_slot = iota((n, D), 1) // 32
    for t in range(out_ref.shape[0]):
        outs = []
        masses = []
        for j in range(2):
            at = pos[:, 2 * t + j : 2 * t + j + 1]
            chip = at >> 5
            where = chip * RET + (at & 31)
            pick = ones_where(iota((n, all_rows.shape[0]), 1) == where)
            outs.append(dot(pick, all_rows))
            mass_at = chip * 8 + ((at >> 3) & 3)
            pick = ones_where(iota((n, mass_rows.shape[0]), 1) == mass_at)
            mass = jnp.where(lane_slot == (at & 7), dot(pick, mass_rows), 0.0).astype(bf16)
            masses.append(dot(mass, widen))
        top = jnp.maximum(masses[0], masses[1])
        w0 = jnp.exp2(masses[0] - top)
        w1 = jnp.exp2(masses[1] - top)
        out_ref[t] = ((w0 * outs[0] + w1 * outs[1]) / (w0 + w1)).astype(bf16)


def vmem_specs(count):
    return [pl.BlockSpec(memory_space=pltpu.VMEM) for _ in range(count)]


def body(queries, probes, keys, values, bucket_home, bucket_rows):
    chips = lax.axis_size("y") * lax.axis_size("col")
    core = lax.axis_index("core")
    device = lax.axis_index(("y", "core", "col"))
    partner = device + jnp.where(core == 0, 16, -16)
    swap = [(0, 1), (1, 0)]
    k_own, v_own = keys[0], values[0]
    k_other = lax.ppermute(k_own, "core", swap)
    v_other = lax.ppermute(v_own, "core", swap)
    rows_own = jnp.sum(jnp.where(bucket_home == device, bucket_rows, 0))
    rows_other = jnp.sum(jnp.where(bucket_home == partner, bucket_rows, 0))
    info = jnp.stack([core.astype(i32), rows_own, rows_other, jnp.int32(0)])

    steps = queries.shape[0]
    send, pos = pl.pallas_call(
        dispatch_kernel,
        out_shape=(
            jax.ShapeDtypeStruct((chips * 2 * CAP, D), bf16),
            jax.ShapeDtypeStruct((2 * steps, 128), i32),
        ),
        in_specs=vmem_specs(3),
        out_specs=tuple(vmem_specs(2)),
        name="dispatch",
    )(probes.transpose(0, 2, 1), bucket_home.reshape(1, 128), queries)
    recv = lax.all_to_all(
        send.reshape(chips, 2 * CAP, D), ("y", "col"), split_axis=0, concat_axis=0, tiled=True
    )
    kt, vbd, mean = pl.pallas_call(
        prepare_kernel,
        out_shape=(
            jax.ShapeDtypeStruct((2, 4, D, KB), bf16),
            jax.ShapeDtypeStruct((2, 2, 4, 4 * KB, 256), bf16),
            jax.ShapeDtypeStruct((2, 8, D), f32),
        ),
        in_specs=[pl.BlockSpec(memory_space=pltpu.SMEM)] + vmem_specs(4),
        out_specs=tuple(vmem_specs(3)),
        name="prepare",
    )(info, k_own, v_own, k_other, v_other)
    padded = chips * CAP + QB
    ret = pl.pallas_call(
        attention_kernel,
        out_shape=jax.ShapeDtypeStruct((chips, RET, D), bf16),
        in_specs=[pl.BlockSpec(memory_space=pltpu.SMEM)] + vmem_specs(4),
        out_specs=vmem_specs(1)[0],
        scratch_shapes=[
            pltpu.VMEM((2, padded, D), bf16),
            pltpu.VMEM((2, padded, D), bf16),
            pltpu.VMEM((2, padded, 128), bf16),
            pltpu.VMEM((2, chips // 8, 128, 128), bf16),
            pltpu.VMEM((2, chips // 8, 128, 128), bf16),
            pltpu.VMEM((H, QB, 128), bf16),
            pltpu.VMEM((2, QB, 256), f32),
            pltpu.VMEM((2, QB, 128), f32),
        ],
        name="attention",
    )(info, recv, kt, vbd, mean)
    back = lax.all_to_all(ret, ("y", "col"), split_axis=0, concat_axis=0, tiled=True)
    return pl.pallas_call(
        combine_kernel,
        out_shape=jax.ShapeDtypeStruct(queries.shape, bf16),
        in_specs=vmem_specs(2),
        out_specs=vmem_specs(1)[0],
        name="combine",
    )(pos, back)


def solution(mesh):
    split = Mesh(mesh.devices.reshape(mesh.devices.shape[0] // 2, 2, mesh.devices.shape[1]), ("y", "core", "col"))
    every = ("y", "core", "col")
    return jax.shard_map(
        body,
        mesh=split,
        in_specs=(
            P(None, every, None),
            P(None, every, None),
            P(every, None, None),
            P(every, None, None),
            P(),
            P(),
        ),
        out_specs=P(None, every, None),
        check_vma=False,
    )
```

```python
import math

import jax
import jax.numpy as jnp
from jax import lax
from jax.experimental import pallas as pl
from jax.experimental.pallas import tpu as pltpu
from jax.sharding import Mesh, PartitionSpec as P

H = 8
HD = 32
D = 256
KB = 256
CAP = 16
RET = 40
SCALE2 = math.log2(math.e) / math.sqrt(HD)
SAFE = 60.0
NORMS = (SAFE / SCALE2) ** 2 / 1.05

f32 = jnp.float32
bf16 = jnp.bfloat16
i32 = jnp.int32


def iota(shape, dim):
    return lax.broadcasted_iota(i32, shape, dim)


def dot(a, b):
    return jnp.dot(a, b, preferred_element_type=f32)


def dot_t(a, b):
    return lax.dot_general(a, b, (((1,), (1,)), ((), ())), preferred_element_type=f32)


def ones_where(cond):
    return jnp.where(cond, 1.0, 0.0).astype(bf16)


def pick_rows(index, shape):
    along = 1 if index.shape[1] == 1 else 0
    grid = iota(shape, along).astype(f32).astype(bf16)
    return jnp.where(grid == index.astype(bf16), jnp.ones(shape, bf16), jnp.zeros(shape, bf16))


def dispatch_kernel(probes_ref, home_ref, q_ref, send_ref, pos_ref):
    steps = probes_ref.shape[0]
    n = 128
    eye = iota((n, n), 0) == iota((n, n), 1)
    home_row = jnp.broadcast_to(home_ref[...].astype(f32), (n, n))
    home = dot(jnp.where(eye, home_row, 0.0).astype(bf16), jnp.ones((n, n), bf16)).astype(i32)
    core = (home >> 4) & 1
    chip = ((home >> 5) << 4) + (home & 15)
    base = (chip * (2 * CAP) + core * CAP).astype(f32)
    tri = jnp.concatenate(
        [ones_where(iota((n, n), 0) < iota((n, n), 1)), jnp.ones((n, n), bf16)], axis=1
    )
    bucket = iota((n, n), 0)
    hits = [[bucket == probes_ref[t, j : j + 1, :] for j in range(2)] for t in range(steps)]
    counts = [[dot(ones_where(hit), tri) for hit in pair] for pair in hits]
    pos_rows = []
    for t in range(steps):
        for j in range(2):
            mine = jnp.where(hits[t][j], counts[t][j][:, :n] + base, 0.0)
            pos_rows.append(jnp.sum(mine, axis=0, keepdims=True))
            base = base + counts[t][j][:, n:]
    pos = jnp.concatenate(pos_rows, axis=0)
    pos_ref[...] = pos
    rows = 256
    queries = q_ref[...].reshape(steps * n, D)
    first = jnp.concatenate([pos[2 * t : 2 * t + 1] for t in range(steps)], axis=1)
    second = jnp.concatenate([pos[2 * t + 1 : 2 * t + 2] for t in range(steps)], axis=1)
    for block in range(send_ref.shape[0] * 2 * CAP // rows):
        pick = pick_rows(first - block * rows, (rows, steps * n)) + pick_rows(
            second - block * rows, (rows, steps * n)
        )
        out = dot(pick, queries).astype(bf16)
        chips = rows // (2 * CAP)
        send_ref[block * chips : (block + 1) * chips] = out.reshape(chips, 2 * CAP, D)


def bucket_sizes(home_ref, rows_ref):
    core = lax.axis_index("core")
    columns = lax.axis_size("col")
    device = (lax.axis_index("y") * 2 + core) * columns + lax.axis_index("col")
    partner = device + columns * (1 - 2 * core)
    rows = rows_ref[...].astype(f32)

    def size(where):
        return jnp.sum(jnp.where(home_ref[...] == where, rows, 0.0)).astype(i32)

    return core, size(device), size(partner)


def prepare_kernel(home_ref, rows_ref, k_own, v_own, k_other, v_other, kt_ref, v_ref, stat_ref):
    _, own, other = bucket_sizes(home_ref, rows_ref)
    head_sum = ones_where((iota((D, 128), 0) // HD) == iota((D, 128), 1))
    for u in range(2):
        key_ref = (k_own, k_other)[u]
        value_ref = (v_own, v_other)[u]
        count = (own, other)[u]
        total = jnp.zeros((8, D), f32)
        norm = jnp.zeros((KB, 128), f32)
        for kb in range(1024 // KB):
            key = key_ref[kb * KB : (kb + 1) * KB, :]
            kt_ref[u, kb] = key.T
            value = value_ref[kb * KB : (kb + 1) * KB, :]
            v_ref[u, kb] = value
            valid = (iota((8, KB), 1) + kb * KB) < count
            total = total + dot(ones_where(valid), value)
            norm = jnp.maximum(norm, dot(key * key, head_sum))
        stat_ref[u, 0:8, :] = total
        stat_ref[u, 8:16, :] = jnp.full((8, D), jnp.max(norm), f32)


def attention_kernel(
    home_ref, rows_ref, recv_ref, kt_ref, v_ref, stat_ref, ret_ref,
    qc_ref, oc_ref, wc_ref, acc_ref, max_ref,
):
    n = 256
    groups = recv_ref.shape[0] * CAP // n
    srcs = n // CAP
    core, own, other = bucket_sizes(home_ref, rows_ref)

    def key_count(u):
        return jnp.where(u == 0, own, other)

    def slots(j, g):
        return recv_ref[srcs * g : srcs * (g + 1), j * CAP : (j + 1) * CAP, :].reshape(n, D)

    total_groups = 2 * groups
    row = iota((16, n), 0)
    live = jnp.zeros((16, n), f32)
    head_sum = ones_where((iota((D, 128), 0) // HD) == iota((D, 128), 1))
    largest = jnp.zeros((n, 128), f32)
    for j in range(2):
        for g in range(groups):
            q = slots(j, g)
            used = jnp.where(q != 0, jnp.ones((n, D), bf16), jnp.zeros((n, D), bf16))
            live = jnp.where(row == j * groups + g, dot_t(jnp.ones((16, D), bf16), used), live)
            largest = jnp.maximum(largest, dot(q * q, head_sum))
    live = live > 0.5
    upper = ones_where(iota((n, n), 0) < iota((n, n), 1))
    rank = dot(ones_where(live), upper)
    code = jnp.where(live, rank, -1.0)
    code_t = code.T
    sizes = jnp.sum(jnp.where(live, 1.0, 0.0), axis=1, keepdims=True).astype(i32)
    offsets = []
    ends = []
    for j in range(2):
        offset = jnp.int32(0)
        for g in range(groups):
            index = j * groups + g
            offsets.append(pl.multiple_of(offset, 16))
            offset = offset + ((sizes[index, 0] + 15) >> 4) * 16
        ends.append(offset)
    for j in range(2):
        for g in range(groups):
            index = j * groups + g
            gather = pick_rows(code[index : index + 1, :], (n, n))
            qc_ref[j, pl.ds(offsets[index], n), :] = dot(gather, slots(j, g)).astype(bf16)
    keys_norm = jnp.maximum(stat_ref[0, 8:9, 0:128], stat_ref[1, 8:9, 0:128])
    fast = jnp.max(largest * keys_norm) <= NORMS

    def masked_keys(u, kb, h):
        g, hh = h // 4, h % 4
        part = kt_ref[u, kb, h * HD : (h + 1) * HD, :]
        pieces = [part if k == hh else jnp.zeros((HD, KB), bf16) for k in range(4)]
        return jnp.concatenate(pieces, axis=0)

    lane = iota((KB, 128), 1)
    in_head = [(lane >= hh * HD) & (lane < (hh + 1) * HD) for hh in range(4)]
    zeros = jnp.zeros((KB, 128), bf16)
    ones = jnp.ones((KB, 128), bf16)

    def head_values(u, kb, h):
        g, hh = h // 4, h % 4
        part = jnp.where(in_head[hh], v_ref[u, kb, :, g * 128 : (g + 1) * 128], zeros)
        return jnp.concatenate([part, jnp.where(in_head[hh], ones, zeros)], axis=1)

    def finish(j, start, rows, values, totals, maxima):
        lanes = iota((rows, 128), 1)
        out = None
        for g in range(2):
            oc_ref[j, pl.ds(start, rows), g * 128 : (g + 1) * 128] = values[g].astype(bf16)
            high = totals[g].astype(bf16)
            mid = (totals[g] - high.astype(f32)).astype(bf16)
            w = jnp.where(lanes % 4 == 0, high.astype(f32), mid.astype(f32))
            if maxima is None:
                w = jnp.where(lanes % 4 < 2, w, 0.0)
            else:
                top, rest = maxima[g]
                w = jnp.where(lanes % 4 == 2, top, w)
                w = jnp.where(lanes % 4 == 3, rest, w)
            out = w if out is None else jnp.where(lanes % 8 < 4, out, w)
        wc_ref[j, pl.ds(start, rows), :] = out.astype(bf16)

    def fast_chunk(j, u, start, rows, blocks, keys):
        acc_ref[:, 0:rows, :] = jnp.zeros((2, rows, D), f32)

        def block(kb, carry):
            valid = ones_where((iota((1, KB), 1) + kb * KB) < keys)
            for g in range(2):
                q = qc_ref[j, pl.ds(start, rows), g * 128 : (g + 1) * 128]
                total = acc_ref[g, 0:rows, :]
                for hh in range(4):
                    s = dot(q, masked_keys(u, kb, 4 * g + hh))
                    p = jnp.exp2(s * SCALE2).astype(bf16) * valid
                    total = total + dot(p, head_values(u, kb, 4 * g + hh))
                acc_ref[g, 0:rows, :] = total
            return carry

        lax.fori_loop(0, blocks, block, 0)
        finish(
            j, start, rows,
            [acc_ref[g, 0:rows, 0:128] for g in range(2)],
            [acc_ref[g, 0:rows, 128:256] for g in range(2)],
            None,
        )

    def slow_chunk(j, u, start, rows, blocks, keys):
        acc_ref[:, 0:rows, :] = jnp.zeros((2, rows, D), f32)
        max_ref[...] = jnp.full(max_ref.shape, -3e38, f32)
        lanes = iota((rows, 128), 1)

        def scores(h, kb):
            g = h // 4
            q = qc_ref[j, pl.ds(start, rows), g * 128 : (g + 1) * 128]
            s = dot(q, masked_keys(u, kb, h)) * SCALE2
            return s, (iota((rows, KB), 1) + kb * KB) < keys

        def find(kb, carry):
            for h in range(H):
                g, hh = h // 4, h % 4
                mine = (lanes >= hh * HD) & (lanes < (hh + 1) * HD)
                s, valid = scores(h, kb)
                top = jnp.max(jnp.where(valid, s, -3e38), axis=1, keepdims=True)
                max_ref[g] = jnp.where(mine, jnp.maximum(max_ref[g], top), max_ref[g])
            return carry

        def block(kb, carry):
            for h in range(H):
                g, hh = h // 4, h % 4
                mine = (lanes >= hh * HD) & (lanes < (hh + 1) * HD)
                s, valid = scores(h, kb)
                top = jnp.max(jnp.where(mine, max_ref[g], -3e38), axis=1, keepdims=True)
                p = jnp.where(valid, jnp.exp2(s - top), 0.0).astype(bf16)
                acc_ref[g, 0:rows, :] += dot(p, head_values(u, kb, h))
            return carry

        lax.fori_loop(0, blocks, find, 0)
        lax.fori_loop(0, blocks, block, 0)
        values, totals, maxima = [], [], []
        for g in range(2):
            total = acc_ref[g, 0:rows, 128:256]
            values.append(acc_ref[g, 0:rows, 0:128] / total)
            mass = jnp.log2(total) + max_ref[g]
            top = mass.astype(bf16).astype(f32)
            rest = (mass - top).astype(bf16).astype(f32)
            totals.append(jnp.exp2(mass - top - rest))
            maxima.append((top, rest))
        finish(j, start, rows, values, totals, maxima)

    def per_bucket(j, carry):
        u = j ^ core
        keys = key_count(u)
        blocks = (keys + KB - 1) // KB
        end = jnp.where(j == 0, ends[0], ends[1])
        rest = ((end & 511) + 127) >> 7
        big = (end >> 9) + jnp.where(rest == 4, 1, 0)
        half = jnp.where((rest == 2) | (rest == 3), 1, 0)
        small = jnp.where((rest == 1) | (rest == 3), 1, 0)

        @pl.when(fast)
        def _():
            def chunk(ch, carry):
                fast_chunk(j, u, pl.multiple_of(ch * 512, 128), 512, blocks, keys)
                return carry

            lax.fori_loop(0, big, chunk, 0)

            @pl.when(half == 1)
            def _():
                fast_chunk(j, u, pl.multiple_of(big * 512, 128), 256, blocks, keys)

            @pl.when(small == 1)
            def _():
                fast_chunk(j, u, pl.multiple_of(big * 512 + half * 256, 128), 128, blocks, keys)

        @pl.when(jnp.logical_not(fast))
        def _():
            def chunk(ch, carry):
                slow_chunk(j, u, pl.multiple_of(ch * 128, 128), 128, blocks, keys)
                return carry

            lax.fori_loop(0, 4 * big + 2 * half + small, chunk, 0)

        done = pl.multiple_of(big * 512 + half * 256 + small * 128, 128)
        oc_ref[j, pl.ds(done, n), :] = jnp.zeros((n, D), bf16)
        wc_ref[j, pl.ds(done, n), :] = jnp.zeros((n, 128), bf16)
        return carry

    lax.fori_loop(0, 2, per_bucket, 0)

    lane_in = iota((128, D), 0)
    lane_out = iota((128, D), 1) % 32
    spread = ones_where(lane_in == (lane_out >> 3) * HD + (lane_out & 7))
    own_lanes = (iota((n, D), 1) // 32) == (iota((n, D), 0) % 8)
    lanes = iota((1, 128), 1)
    for g in range(groups):
        mass_rows = jnp.zeros((srcs * 8, D), f32)
        for j in range(2):
            index = j * groups + g
            u = j ^ core
            count = key_count(u).astype(f32)
            count_row = jnp.full((1, 128), count, f32)
            count_high = count_row.astype(bf16).astype(f32)
            zero_mass = jnp.where(lanes % 4 == 0, count_high, jnp.where(lanes % 4 == 1, count_row - count_high, 0.0))
            column = code_t[:, index : index + 1]
            dead = column < 0.0
            scatter = pick_rows(column, (n, n))
            rows = dot(scatter, oc_ref[j, pl.ds(offsets[index], n), :])
            rows = jnp.where(dead, stat_ref[u, 0:1, :], rows).astype(bf16)
            ret_ref[srcs * g : srcs * (g + 1), j * CAP : (j + 1) * CAP, :] = rows.reshape(srcs, CAP, D)
            mass = dot(scatter, wc_ref[j, pl.ds(offsets[index], n), :])
            mass = jnp.where(dead, zero_mass, mass).astype(bf16)
            wide = jnp.where(own_lanes, dot(mass, spread), 0.0).astype(bf16)
            out_row = iota((srcs * 8, n), 0)
            slot = iota((srcs * 8, n), 1)
            mass_rows = mass_rows + dot(
                ones_where(out_row == (slot // 16) * 8 + 2 * j + (slot % 16) // 8), wide
            )
        ret_ref[srcs * g : srcs * (g + 1), 32:40, :] = mass_rows.astype(bf16).reshape(srcs, 8, D)


def combine_kernel(pos_ref, ret_ref, out_ref):
    n = 128
    steps = out_ref.shape[0]
    chips = ret_ref.shape[0]
    pos = pos_ref[...].T
    at = jnp.concatenate([pos[:, 2 * t + j : 2 * t + j + 1] for j in range(2) for t in range(steps)], axis=0)
    at_int = at.astype(i32)
    probes = 2 * steps * n
    per = 256 // (2 * CAP)
    values = jnp.zeros((probes, D), f32)
    for block in range(chips // per):
        rows = ret_ref[block * per : (block + 1) * per, 0:32, :].reshape(256, D)
        values = values + dot(pick_rows(at - block * 256, (probes, 256)), rows)
    mass_at = ((at_int >> 5) * 8 + ((at_int >> 3) & 3)).astype(f32)
    mass = jnp.zeros((probes, D), f32)
    for block in range(chips // 32):
        rows = ret_ref[block * 32 : (block + 1) * 32, 32:40, :].reshape(256, D)
        mass = mass + dot(pick_rows(mass_at - block * 256, (probes, 256)), rows)
    mass = jnp.where((iota((probes, D), 1) // 32) == (at_int & 7), mass, 0.0).astype(bf16)
    lane_in = iota((D, D), 0) % 32
    head = iota((D, D), 1) // HD
    same_head = ((lane_in >> 3) == (head & 3)) & (((lane_in >> 2) & 1) == (head >> 2))
    total = dot(mass, ones_where(same_head & ((lane_in & 3) < 2)))
    top = dot(mass, ones_where(same_head & ((lane_in & 3) >= 2)))
    half = steps * n
    highest = jnp.maximum(top[:half], top[half:])
    w0 = jnp.exp2(top[:half] - highest)
    w1 = jnp.exp2(top[half:] - highest)
    merged = (w0 * values[:half] + w1 * values[half:]) / (w0 * total[:half] + w1 * total[half:])
    out_ref[...] = merged.astype(bf16).reshape(steps, n, D)


def near(x):
    return pltpu.with_memory_space_constraint(x, pltpu.VMEM)


def call(kernel, name, mib, outs, args, scratch=()):
    spec = pl.BlockSpec(memory_space=pltpu.VMEM)
    single = not isinstance(outs, tuple)
    return pl.pallas_call(
        kernel,
        out_shape=outs,
        in_specs=[spec] * len(args),
        out_specs=spec if single else tuple(spec for _ in outs),
        scratch_shapes=list(scratch),
        compiler_params=pltpu.CompilerParams(vmem_limit_bytes=mib << 20),
        name=name,
    )(*args)


def body(queries, probes, keys, values, bucket_home, bucket_rows):
    chips = lax.axis_size("y") * lax.axis_size("col")
    steps = queries.shape[0]
    swap = [(0, 1), (1, 0)]
    k_own, v_own = keys[0], values[0]
    k_other = lax.ppermute(k_own, "core", swap)
    v_other = lax.ppermute(v_own, "core", swap)
    home = bucket_home.reshape(1, 128)
    rows = bucket_rows.reshape(1, 128)
    send, pos = call(
        dispatch_kernel, "dispatch", 16,
        (pltpu.VMEM((chips, 2 * CAP, D), bf16), pltpu.VMEM((2 * steps, 128), f32)),
        (probes.transpose(0, 2, 1), home, queries),
    )
    recv = lax.all_to_all(send, ("y", "col"), split_axis=0, concat_axis=0, tiled=True)
    kt, v, stat = call(
        prepare_kernel, "prepare", 16,
        (
            pltpu.VMEM((2, 4, D, KB), bf16),
            pltpu.VMEM((2, 4, KB, D), bf16),
            pltpu.VMEM((2, 16, D), f32),
        ),
        (home, rows, k_own, v_own, k_other, v_other),
    )
    padded = chips * CAP + 256
    ret = call(
        attention_kernel, "attention", 24,
        pltpu.VMEM((chips, RET, D), bf16),
        (home, rows, near(recv), near(kt), near(v), near(stat)),
        (
            pltpu.VMEM((2, padded, D), bf16),
            pltpu.VMEM((2, padded, D), bf16),
            pltpu.VMEM((2, padded, 128), bf16),
            pltpu.VMEM((2, 512, D), f32),
            pltpu.VMEM((2, 128, 128), f32),
        ),
    )
    back = lax.all_to_all(ret, ("y", "col"), split_axis=0, concat_axis=0, tiled=True)
    return call(
        combine_kernel, "combine", 24,
        jax.ShapeDtypeStruct(queries.shape, bf16),
        (near(pos), near(back)),
    )


def solution(mesh):
    rows, columns = mesh.devices.shape
    split = Mesh(mesh.devices.reshape(rows // 2, 2, columns), ("y", "core", "col"))
    every = ("y", "core", "col")
    return jax.shard_map(
        body,
        mesh=split,
        in_specs=(
            P(None, every, None),
            P(None, every, None),
            P(every, None, None),
            P(every, None, None),
            P(),
            P(),
        ),
        out_specs=P(None, every, None),
        check_vma=False,
    )
```

```python
import math

import jax
import jax.numpy as jnp
from jax import lax
from jax.experimental import pallas as pl
from jax.experimental.pallas import tpu as pltpu
from jax.sharding import Mesh, PartitionSpec as P

H = 8
HD = 32
D = 256
KB = 256
SLOTS = 32
RET = 72
SCALE2 = math.log2(math.e) / math.sqrt(HD)
SAFE = 80.0
NORMS = (SAFE / SCALE2) ** 2 / 1.05

f32 = jnp.float32
bf16 = jnp.bfloat16
i32 = jnp.int32


def iota(shape, dim):
    return lax.broadcasted_iota(i32, shape, dim)


def dot(a, b):
    return jnp.dot(a, b, preferred_element_type=f32)


def dot_t(a, b):
    return lax.dot_general(a, b, (((1,), (1,)), ((), ())), preferred_element_type=f32)


def ones_where(cond):
    return jnp.where(cond, 1.0, 0.0).astype(bf16)


def pick_rows(index, shape):
    along = 1 if index.shape[1] == 1 else 0
    grid = iota(shape, along).astype(f32).astype(bf16)
    return jnp.where(grid == index.astype(bf16), jnp.ones(shape, bf16), jnp.zeros(shape, bf16))


def dispatch_kernel(probes_hbm, home_hbm, q_hbm, send_hbm, pos_ref, probes_ref, home_ref, q_ref, send_ref, in_sem, out_sem):
    copies = [
        pltpu.make_async_copy(source, target, in_sem.at[k])
        for k, (source, target) in enumerate(((home_hbm, home_ref), (probes_hbm, probes_ref), (q_hbm, q_ref)))
    ]
    for copy in copies:
        copy.start()
    steps = probes_ref.shape[0]
    n = 128
    tri = jnp.concatenate(
        [ones_where(iota((n, n), 0) < iota((n, n), 1)), jnp.ones((n, n), bf16)], axis=1
    )
    eye = iota((n, n), 0) == iota((n, n), 1)
    bucket = iota((n, n), 0)
    copies[0].wait()
    home_row = jnp.broadcast_to(home_ref[...].astype(f32), (n, n))
    home = dot(jnp.where(eye, home_row, 0.0).astype(bf16), jnp.ones((n, n), bf16)).astype(i32)
    core = (home >> 4) & 1
    chip = ((home >> 5) << 4) + (home & 15)
    base = (chip * SLOTS + core * 4).astype(f32)
    copies[1].wait()
    hits = [[bucket == probes_ref[t, j : j + 1, :] for j in range(2)] for t in range(steps)]
    counts = [[dot(ones_where(hit), tri) for hit in pair] for pair in hits]
    pos_rows = []
    for t in range(steps):
        before = base + 8.0 * t
        for j in range(2):
            mine = jnp.where(hits[t][j], counts[t][j][:, :n] + before, 0.0)
            pos_rows.append(jnp.sum(mine, axis=0, keepdims=True))
            before = before + counts[t][j][:, n:]
    pos = jnp.concatenate(pos_rows, axis=0)
    pos_ref[...] = pos
    rows = 256
    first = jnp.concatenate([pos[2 * t : 2 * t + 1] for t in range(steps)], axis=1)
    second = jnp.concatenate([pos[2 * t + 1 : 2 * t + 2] for t in range(steps)], axis=1)
    copies[2].wait()
    queries = q_ref[...].reshape(steps * n, D)
    chips = rows // SLOTS
    out_copies = []
    for block in range(send_ref.shape[0] // chips):
        pick = pick_rows(first - block * rows, (rows, steps * n)) + pick_rows(
            second - block * rows, (rows, steps * n)
        )
        out = dot(pick, queries).astype(bf16)
        part = pl.ds(block * chips, chips)
        send_ref[block * chips : (block + 1) * chips] = out.reshape(chips, SLOTS, D)
        out_copies.append(pltpu.make_async_copy(send_ref.at[part], send_hbm.at[part], out_sem.at[block]))
        out_copies[-1].start()
    for copy in out_copies:
        copy.wait()


def bucket_sizes(home_ref, rows_ref):
    core = lax.axis_index("core")
    columns = lax.axis_size("col")
    device = (lax.axis_index("y") * 2 + core) * columns + lax.axis_index("col")
    partner = device + columns * (1 - 2 * core)
    rows = rows_ref[...].astype(f32)

    def size(where):
        return jnp.sum(jnp.where(home_ref[...] == where, rows, 0.0)).astype(i32)

    return core, size(device), size(partner)


def prepare_kernel(home_ref, rows_ref, k_own, v_own, k_other, v_other, kt_ref, v_ref, stat_ref):
    _, own, other = bucket_sizes(home_ref, rows_ref)
    head_sum = ones_where((iota((D, 128), 0) // HD) == iota((D, 128), 1))
    for u in range(2):
        key_ref = (k_own, k_other)[u]
        value_ref = (v_own, v_other)[u]
        count = (own, other)[u]
        total = jnp.zeros((8, D), f32)
        norm = jnp.zeros((KB, 128), f32)
        for kb in range(1024 // KB):
            key = key_ref[kb * KB : (kb + 1) * KB, :]
            kt_ref[u, kb] = key.T
            value = value_ref[kb * KB : (kb + 1) * KB, :]
            v_ref[u, kb] = value
            valid = (iota((8, KB), 1) + kb * KB) < count
            total = total + dot(ones_where(valid), value)
            norm = jnp.maximum(norm, dot(key * key, head_sum))
        stat_ref[u, 0:8, :] = total
        stat_ref[u, 8:16, :] = jnp.full((8, D), jnp.max(norm), f32)


def attention_kernel(
    home_ref, rows_ref, recv_ref, kt_ref, v_ref, stat_ref, ret_ref,
    qc_ref, oc_ref, wc_ref, acc_ref, max_ref,
):
    n = 256
    half = n // 2
    srcs = n // SLOTS
    groups = recv_ref.shape[0] // srcs
    core, own, other = bucket_sizes(home_ref, rows_ref)

    def key_count(u):
        return jnp.where(u == 0, own, other)

    def slots(g):
        return recv_ref[srcs * g : srcs * (g + 1)].reshape(n, D)

    row = iota((groups, n), 0)
    side = (iota((1, n), 1) >> 2) & 1
    heads = ones_where((iota((16, D), 1) // HD) == iota((16, D), 0))
    norm = jnp.zeros((groups, n), f32)
    unsafe = jnp.zeros((8, n), f32)
    keys_norm = jnp.maximum(stat_ref[0, 8:9, :], stat_ref[1, 8:9, :])
    for g in range(groups):
        q = slots(g)
        squares = dot_t(heads, q * q)[0:8, :]
        unsafe = jnp.maximum(unsafe, jnp.where(squares * keys_norm <= NORMS, 0.0, 1.0))
        norm = jnp.where(row == g, jnp.sum(squares, axis=0, keepdims=True), norm)
    live = jnp.where(norm <= 0.0, 0.0, 1.0)
    side_in = (iota((n, n), 0) >> 2) & 1
    side_out = (iota((n, n), 1) >> 2) & 1
    upper = ones_where((iota((n, n), 0) < iota((n, n), 1)) & (side_in == side_out))
    rank = dot(live.astype(bf16), upper)
    code = jnp.where(live > 0.5, rank + (side * half).astype(f32), -1.0)
    code_t = code.T
    offsets = [[], []]
    ends = []
    for j in range(2):
        sizes = jnp.sum(jnp.where(side == j, live, 0.0), axis=1, keepdims=True).astype(i32)
        offset = jnp.int32(0)
        for g in range(groups):
            offsets[j].append(pl.multiple_of(offset, 16))
            offset = offset + ((sizes[g, 0] + 15) >> 4) * 16
        ends.append(offset)
    for g in range(groups):
        rows = dot(pick_rows(code[g : g + 1, :], (n, n)), slots(g)).astype(bf16)
        for j in range(2):
            qc_ref[j, pl.ds(offsets[j][g], half), :] = rows[j * half : (j + 1) * half]
    fast = jnp.max(unsafe) < 0.5

    def masked_keys(u, kb, h):
        g, hh = h // 4, h % 4
        part = kt_ref[u, kb, h * HD : (h + 1) * HD, :]
        pieces = [part if k == hh else jnp.zeros((HD, KB), bf16) for k in range(4)]
        return jnp.concatenate(pieces, axis=0)

    lane = iota((KB, 128), 1)
    in_head = [(lane >= hh * HD) & (lane < (hh + 1) * HD) for hh in range(4)]
    zeros = jnp.zeros((KB, 128), bf16)
    ones = jnp.ones((KB, 128), bf16)

    total_lanes = [[ones_where((lane & 28) == 8 * hh + 4 * g) for hh in range(4)] for g in range(2)]

    def head_values(u, kb, h):
        g, hh = h // 4, h % 4
        part = jnp.where(in_head[hh], v_ref[u, kb, :, g * 128 : (g + 1) * 128], zeros)
        return jnp.concatenate([part, total_lanes[g][hh]], axis=1)

    def finish(j, start, rows, values, total, maxima):
        lanes = iota((rows, 128), 1) & 3
        for g in range(2):
            oc_ref[j, pl.ds(start, rows), g * 128 : (g + 1) * 128] = values[g].astype(bf16)
        high = total.astype(bf16).astype(f32)
        w = jnp.where(lanes == 0, high, total - high)
        if maxima is None:
            w = jnp.where(lanes < 2, w, 0.0)
        else:
            top, rest = maxima
            w = jnp.where(lanes == 2, top, w)
            w = jnp.where(lanes == 3, rest, w)
        wc_ref[j, pl.ds(start, rows), :] = w.astype(bf16)

    def fast_chunk(j, u, start, rows, blocks, keys):
        acc_ref[:, 0:rows, :] = jnp.zeros((2, rows, D), f32)

        def block(kb, carry):
            valid = ones_where((iota((1, KB), 1) + kb * KB) < keys)
            for g in range(2):
                q = qc_ref[j, pl.ds(start, rows), g * 128 : (g + 1) * 128]
                total = acc_ref[g, 0:rows, :]
                for hh in range(4):
                    s = dot(q, masked_keys(u, kb, 4 * g + hh))
                    p = jnp.exp2(s * SCALE2).astype(bf16) * valid
                    total = total + dot(p, head_values(u, kb, 4 * g + hh))
                acc_ref[g, 0:rows, :] = total
            return carry

        lax.fori_loop(0, blocks, block, 0)
        finish(
            j, start, rows,
            [acc_ref[g, 0:rows, 0:128] for g in range(2)],
            acc_ref[0, 0:rows, 128:256] + acc_ref[1, 0:rows, 128:256],
            None,
        )

    def slow_chunk(j, u, start, rows, blocks, keys):
        acc_ref[:, 0:rows, :] = jnp.zeros((2, rows, D), f32)
        max_ref[...] = jnp.full(max_ref.shape, -3e38, f32)
        lanes = iota((rows, 128), 1)

        def scores(h, kb):
            g = h // 4
            q = qc_ref[j, pl.ds(start, rows), g * 128 : (g + 1) * 128]
            s = dot(q, masked_keys(u, kb, h)) * SCALE2
            return s, (iota((rows, KB), 1) + kb * KB) < keys

        def find(kb, carry):
            for h in range(H):
                g, hh = h // 4, h % 4
                mine = (lanes >= hh * HD) & (lanes < (hh + 1) * HD)
                s, valid = scores(h, kb)
                top = jnp.max(jnp.where(valid, s, -3e38), axis=1, keepdims=True)
                max_ref[g] = jnp.where(mine, jnp.maximum(max_ref[g], top), max_ref[g])
            return carry

        def block(kb, carry):
            for h in range(H):
                g, hh = h // 4, h % 4
                mine = (lanes >= hh * HD) & (lanes < (hh + 1) * HD)
                s, valid = scores(h, kb)
                top = jnp.max(jnp.where(mine, max_ref[g], -3e38), axis=1, keepdims=True)
                p = jnp.where(valid, jnp.exp2(s - top), 0.0).astype(bf16)
                acc_ref[g, 0:rows, :] += dot(p, head_values(u, kb, h))
            return carry

        lax.fori_loop(0, blocks, find, 0)
        lax.fori_loop(0, blocks, block, 0)
        total = acc_ref[0, 0:rows, 128:256] + acc_ref[1, 0:rows, 128:256]
        tops = jnp.zeros((rows, 128), f32)
        values = []
        for g in range(2):
            scale = jnp.zeros((rows, 128), f32)
            for hh in range(4):
                mine = (lanes >= hh * HD) & (lanes < (hh + 1) * HD)
                there = (lanes & 28) == 8 * hh + 4 * g
                mass = jnp.max(jnp.where(there, total, 0.0), axis=1, keepdims=True)
                top = jnp.max(jnp.where(mine, max_ref[g], -3e38), axis=1, keepdims=True)
                scale = jnp.where(mine, mass, scale)
                tops = jnp.where(there, top, tops)
            values.append(acc_ref[g, 0:rows, 0:128] / scale)
        mass = jnp.log2(total) + tops
        top = mass.astype(bf16).astype(f32)
        rest = (mass - top).astype(bf16).astype(f32)
        finish(j, start, rows, values, jnp.exp2(mass - top - rest), (top, rest))

    def per_bucket(j, carry):
        u = j ^ core
        keys = key_count(u)
        blocks = (keys + KB - 1) // KB
        end = jnp.where(j == 0, ends[0], ends[1])
        rest = ((end & 511) + 127) >> 7
        big = (end >> 9) + jnp.where(rest == 4, 1, 0)
        middle = jnp.where((rest == 2) | (rest == 3), 1, 0)
        small = jnp.where((rest == 1) | (rest == 3), 1, 0)

        @pl.when(fast)
        def _():
            def chunk(ch, carry):
                fast_chunk(j, u, pl.multiple_of(ch * 512, 128), 512, blocks, keys)
                return carry

            lax.fori_loop(0, big, chunk, 0)

            @pl.when(middle == 1)
            def _():
                fast_chunk(j, u, pl.multiple_of(big * 512, 128), 256, blocks, keys)

            @pl.when(small == 1)
            def _():
                fast_chunk(j, u, pl.multiple_of(big * 512 + middle * 256, 128), 128, blocks, keys)

        @pl.when(jnp.logical_not(fast))
        def _():
            def chunk(ch, carry):
                slow_chunk(j, u, pl.multiple_of(ch * 128, 128), 128, blocks, keys)
                return carry

            lax.fori_loop(0, 4 * big + 2 * middle + small, chunk, 0)

        done = pl.multiple_of(big * 512 + middle * 256 + small * 128, 128)
        oc_ref[j, pl.ds(done, half), :] = jnp.zeros((half, D), bf16)
        wc_ref[j, pl.ds(done, half), :] = jnp.zeros((half, 128), bf16)
        return carry

    lax.fori_loop(0, 2, per_bucket, 0)

    slot = iota((n, D), 0)
    own_side = ((slot >> 2) & 1) == 0
    first, second = stat_ref[core, 0:1, :], stat_ref[1 - core, 0:1, :]
    zero_rows = jnp.where(own_side, first, second)
    slot = iota((n, 128), 0)
    lanes = iota((n, 128), 1)
    counts = jnp.where(((slot >> 2) & 1) == 0, key_count(core).astype(f32), key_count(1 - core).astype(f32))
    count_high = counts.astype(bf16).astype(f32)
    zero_mass = jnp.where((lanes & 3) == 0, count_high, jnp.where((lanes & 3) == 1, counts - count_high, 0.0))
    own_lanes = (lanes >> 5) == (slot & 3)
    mass_row = iota((8 * srcs, n), 0)
    mass_slot = iota((8 * srcs, n), 1)
    collect = ones_where(mass_row == (mass_slot >> 5) * 8 + ((mass_slot & 31) >> 2))
    for g in range(groups):
        column = jnp.broadcast_to(code_t[:, g : g + 1], (n, 128))
        dead = column < 0.0
        scatter = jnp.concatenate(
            [ones_where(column == lanes.astype(f32)), ones_where(column == (lanes + half).astype(f32))], axis=1
        )
        windows = [pl.ds(offsets[j][g], half) for j in range(2)]
        packed = jnp.concatenate([oc_ref[j, windows[j], :] for j in range(2)], axis=0)
        rows = dot(scatter, packed)
        for k in range(2):
            part = slice(k * 128, (k + 1) * 128)
            out = jnp.where(dead, zero_rows[:, part], rows[:, part]).astype(bf16)
            ret_ref[srcs * g : srcs * (g + 1), k * SLOTS : (k + 1) * SLOTS, :] = out.reshape(srcs, SLOTS, 128)
        packed = jnp.concatenate([wc_ref[j, windows[j], :] for j in range(2)], axis=0)
        mass = jnp.where(dead, zero_mass, dot(scatter, packed))
        mass = jnp.where(own_lanes, mass, 0.0).astype(bf16)
        out = dot(collect, mass).astype(bf16)
        ret_ref[srcs * g : srcs * (g + 1), 2 * SLOTS : 2 * SLOTS + 8, :] = out.reshape(srcs, 8, 128)


def combine_kernel(pos_ref, ret_ref, out_ref):
    n = 128
    steps = out_ref.shape[0]
    chips = ret_ref.shape[0]
    pos = pos_ref[...].T
    lane_in = iota((n, D), 0) & 31
    head = iota((n, D), 1) // HD
    same_head = (lane_in >> 2) == 2 * (head & 3) + (head >> 2)
    widen = jnp.concatenate(
        [ones_where(same_head & ((lane_in & 3) < 2)), ones_where(same_head & ((lane_in & 3) >= 2))], axis=1
    )
    lane_slot = iota((2 * n, 128), 1) >> 5
    masses = ret_ref[:, 2 * SLOTS : 2 * SLOTS + 8, :].reshape(chips * 8, 128)
    for t in range(steps):
        at = jnp.concatenate([pos[:, 2 * t + j : 2 * t + j + 1] for j in range(2)], axis=0).astype(i32)
        chip = at >> 5
        where = (chip * 8 + (at & 7)).astype(f32)
        pick = jnp.concatenate([pick_rows(where - 256 * k, (2 * n, 256)) for k in range(chips * 8 // 256)], axis=1)
        halves = [
            dot(pick, ret_ref[:, k * SLOTS + 8 * t : k * SLOTS + 8 * t + 8, :].reshape(chips * 8, 128))
            for k in range(2)
        ]
        values = jnp.concatenate(halves, axis=1)
        where = (chip * 8 + 2 * t + ((at >> 2) & 1)).astype(f32)
        pick = jnp.concatenate([pick_rows(where - 256 * k, (2 * n, 256)) for k in range(chips * 8 // 256)], axis=1)
        mass = jnp.where(lane_slot == (at & 3), dot(pick, masses), 0.0).astype(bf16)
        wide = dot(mass, widen)
        total, top = wide[:, :D], wide[:, D:]
        highest = jnp.maximum(top[:n], top[n:])
        w0 = jnp.exp2(top[:n] - highest)
        w1 = jnp.exp2(top[n:] - highest)
        merged = (w0 * values[:n] + w1 * values[n:]) / (w0 * total[:n] + w1 * total[n:])
        out_ref[t] = merged.astype(bf16)


def near(x):
    return pltpu.with_memory_space_constraint(x, pltpu.VMEM)


def hbm(x):
    return pltpu.with_memory_space_constraint(x, pltpu.HBM)


def call(kernel, name, mib, outs, args, scratch=()):
    spec = pl.BlockSpec(memory_space=pltpu.VMEM)
    single = not isinstance(outs, tuple)
    return pl.pallas_call(
        kernel,
        out_shape=outs,
        in_specs=[spec] * len(args),
        out_specs=spec if single else tuple(spec for _ in outs),
        scratch_shapes=list(scratch),
        compiler_params=pltpu.CompilerParams(vmem_limit_bytes=mib << 20),
        name=name,
    )(*args)


def body(queries, probes, keys, values, bucket_home, bucket_rows):
    chips = lax.axis_size("y") * lax.axis_size("col")
    steps = queries.shape[0]
    swap = [(0, 1), (1, 0)]
    k_own, v_own = keys[0], values[0]
    k_other = lax.ppermute(k_own, "core", swap)
    v_other = lax.ppermute(v_own, "core", swap)
    home = bucket_home.reshape(1, 128)
    rows = bucket_rows.reshape(1, 128)
    far = pl.BlockSpec(memory_space=pltpu.HBM)
    send, pos = pl.pallas_call(
        dispatch_kernel,
        out_shape=(jax.ShapeDtypeStruct((chips, SLOTS, D), bf16), pltpu.VMEM((2 * steps, 128), f32)),
        in_specs=[far] * 3,
        out_specs=(far, pl.BlockSpec(memory_space=pltpu.VMEM)),
        scratch_shapes=[
            pltpu.VMEM((steps, 2, 128), i32),
            pltpu.VMEM((1, 128), i32),
            pltpu.VMEM(queries.shape, bf16),
            pltpu.VMEM((chips, SLOTS, D), bf16),
            pltpu.SemaphoreType.DMA((3,)),
            pltpu.SemaphoreType.DMA((chips * SLOTS // 256,)),
        ],
        compiler_params=pltpu.CompilerParams(vmem_limit_bytes=16 << 20),
        name="dispatch",
    )(hbm(probes.transpose(0, 2, 1)), hbm(home), hbm(queries))
    recv = lax.all_to_all(send, ("y", "col"), split_axis=0, concat_axis=0, tiled=True)
    kt, v, stat = call(
        prepare_kernel, "prepare", 16,
        (
            pltpu.VMEM((2, 4, D, KB), bf16),
            pltpu.VMEM((2, 4, KB, D), bf16),
            pltpu.VMEM((2, 16, D), f32),
        ),
        (home, rows, hbm(k_own), hbm(v_own), k_other, v_other),
    )
    padded = chips * 16 + 128
    ret = call(
        attention_kernel, "attention", 24,
        pltpu.VMEM((chips, RET, 128), bf16),
        (home, rows, near(recv), near(kt), near(v), near(stat)),
        (
            pltpu.VMEM((2, padded, D), bf16),
            pltpu.VMEM((2, padded, D), bf16),
            pltpu.VMEM((2, padded, 128), bf16),
            pltpu.VMEM((2, 512, D), f32),
            pltpu.VMEM((2, 128, 128), f32),
        ),
    )
    back = lax.all_to_all(ret, ("y", "col"), split_axis=0, concat_axis=0, tiled=True)
    return call(
        combine_kernel, "combine", 24,
        jax.ShapeDtypeStruct(queries.shape, bf16),
        (near(pos), near(back)),
    )


def solution(mesh):
    rows, columns = mesh.devices.shape
    split = Mesh(mesh.devices.reshape(rows // 2, 2, columns), ("y", "core", "col"))
    every = ("y", "core", "col")
    return jax.shard_map(
        body,
        mesh=split,
        in_specs=(
            P(None, every, None),
            P(None, every, None),
            P(every, None, None),
            P(every, None, None),
            P(),
            P(),
        ),
        out_specs=P(None, every, None),
        check_vma=False,
    )
```

```python
import math

import jax
import jax.numpy as jnp
from jax import lax
from jax.experimental import pallas as pl
from jax.experimental.pallas import tpu as pltpu
from jax.sharding import Mesh, PartitionSpec as P

H = 8
HD = 32
D = 256
KB = 256
QB = 256
SLOTS = 32
RET = 72
SCALE2 = math.log2(math.e) / math.sqrt(HD)
TINY = 2.0**-60
SAFE = 80.0
NORMS = (SAFE / SCALE2) ** 2 / 1.05

f32 = jnp.float32
bf16 = jnp.bfloat16
i32 = jnp.int32


def iota(shape, dim):
    return lax.broadcasted_iota(i32, shape, dim)


def dot(a, b):
    return jnp.dot(a, b, preferred_element_type=f32)


def dot_t(a, b):
    return lax.dot_general(a, b, (((1,), (1,)), ((), ())), preferred_element_type=f32)


def ones_where(cond):
    return jnp.where(cond, 1.0, 0.0).astype(bf16)


def pick_rows(index, shape):
    along = 1 if index.shape[1] == 1 else 0
    grid = iota(shape, along).astype(f32).astype(bf16)
    return jnp.where(grid == index.astype(bf16), jnp.ones(shape, bf16), jnp.zeros(shape, bf16))


def dispatch_kernel(probes_hbm, home_hbm, q_hbm, send_hbm, pos_ref, probes_ref, home_ref, q_ref, send_ref, in_sem, out_sem):
    copies = [
        pltpu.make_async_copy(source, target, in_sem.at[k])
        for k, (source, target) in enumerate(((home_hbm, home_ref), (probes_hbm, probes_ref), (q_hbm, q_ref)))
    ]
    for copy in copies:
        copy.start()
    steps = probes_ref.shape[0]
    n = 128
    tri = jnp.concatenate(
        [ones_where(iota((n, n), 0) < iota((n, n), 1)), jnp.ones((n, n), bf16)], axis=1
    )
    eye = iota((n, n), 0) == iota((n, n), 1)
    bucket = iota((n, n), 0)
    copies[0].wait()
    home_row = jnp.broadcast_to(home_ref[...].astype(f32), (n, n))
    home = dot(jnp.where(eye, home_row, 0.0).astype(bf16), jnp.ones((n, n), bf16)).astype(i32)
    core = (home >> 4) & 1
    chip = ((home >> 5) << 4) + (home & 15)
    base = (chip * SLOTS + core * 4).astype(f32)
    copies[1].wait()
    hits = [[bucket == probes_ref[t, j : j + 1, :] for j in range(2)] for t in range(steps)]
    counts = [[dot(ones_where(hit), tri) for hit in pair] for pair in hits]
    pos_rows = []
    for t in range(steps):
        before = base + 8.0 * t
        for j in range(2):
            mine = jnp.where(hits[t][j], counts[t][j][:, :n] + before, 0.0)
            pos_rows.append(jnp.sum(mine, axis=0, keepdims=True))
            before = before + counts[t][j][:, n:]
    pos = jnp.concatenate(pos_rows, axis=0)
    pos_ref[...] = pos
    rows = 256
    first = jnp.concatenate([pos[2 * t : 2 * t + 1] for t in range(steps)], axis=1)
    second = jnp.concatenate([pos[2 * t + 1 : 2 * t + 2] for t in range(steps)], axis=1)
    copies[2].wait()
    queries = q_ref[...].reshape(steps * n, D)
    lead = queries[:, :n]
    tiny = (iota((steps * n, n), 1) == 0) & (jnp.abs(lead.astype(f32)) < TINY)
    queries = jnp.concatenate([jnp.where(tiny, jnp.full(lead.shape, TINY, bf16), lead), queries[:, n:]], axis=1)
    chips = rows // SLOTS
    out_copies = []
    for block in range(send_ref.shape[0] // chips):
        pick = pick_rows(first - block * rows, (rows, steps * n)) + pick_rows(
            second - block * rows, (rows, steps * n)
        )
        out = dot(pick, queries).astype(bf16)
        part = pl.ds(block * chips, chips)
        send_ref[block * chips : (block + 1) * chips] = out.reshape(chips, SLOTS, D)
        out_copies.append(pltpu.make_async_copy(send_ref.at[part], send_hbm.at[part], out_sem.at[block]))
        out_copies[-1].start()
    for copy in out_copies:
        copy.wait()


def bucket_sizes(home_ref, rows_ref):
    core = lax.axis_index("core")
    columns = lax.axis_size("col")
    device = (lax.axis_index("y") * 2 + core) * columns + lax.axis_index("col")
    partner = device + columns * (1 - 2 * core)
    rows = rows_ref[...].astype(f32)

    def size(where):
        return jnp.sum(jnp.where(home_ref[...] == where, rows, 0.0)).astype(i32)

    return core, size(device), size(partner)


def prepare_kernel(home_ref, rows_ref, k_own, v_own, k_other, v_other, k_ref, vt_ref, valid_ref, stat_ref):
    _, own, other = bucket_sizes(home_ref, rows_ref)
    head_sum = ones_where((iota((D, 128), 0) // HD) == iota((D, 128), 1))
    for u in range(2):
        key_ref = (k_own, k_other)[u]
        value_ref = (v_own, v_other)[u]
        count = (own, other)[u]
        norm = jnp.zeros((KB, 128), f32)
        for kb in range(1024 // KB):
            key = key_ref[kb * KB : (kb + 1) * KB, :]
            k_ref[u, kb] = key
            norm = jnp.maximum(norm, dot(key * key, head_sum))
            valid = ones_where((iota((16, KB), 1) + kb * KB) < count)
            valid_ref[u, kb] = valid
            value = value_ref[kb * KB : (kb + 1) * KB, :]
            vt_ref[u, kb] = value.T * valid[0:1, :]
        stat_ref[u] = jnp.full((8, D), jnp.max(norm), f32)


def attention_kernel(
    home_ref, rows_ref, recv_ref, k_ref, vt_ref, valid_ref, stat_ref, ret_ref,
    qc_ref, oc_ref, qt_ref, p_ref, acc_ref, max_ref,
):
    n = 256
    half = n // 2
    srcs = n // SLOTS
    groups = recv_ref.shape[0] // srcs
    core, own, other = bucket_sizes(home_ref, rows_ref)

    def key_count(u):
        return jnp.where(u == 0, own, other)

    def slots(g):
        return recv_ref[srcs * g : srcs * (g + 1)].reshape(n, D)

    row = iota((groups, n), 0)
    side = (iota((1, n), 1) >> 2) & 1
    heads = ones_where((iota((16, D), 1) // HD) == iota((16, D), 0))
    norm = jnp.zeros((groups, n), f32)
    unsafe = jnp.zeros((8, n), f32)
    keys_norm = jnp.maximum(stat_ref[0, 0:1, :], stat_ref[1, 0:1, :])
    for g in range(groups):
        q = slots(g)
        squares = dot_t(heads, q * q)[0:8, :]
        unsafe = jnp.maximum(unsafe, jnp.where(squares * keys_norm <= NORMS, 0.0, 1.0))
        norm = jnp.where(row == g, jnp.sum(squares, axis=0, keepdims=True), norm)
    live = jnp.where(norm <= 0.0, 0.0, 1.0)
    side_in = (iota((n, n), 0) >> 2) & 1
    side_out = (iota((n, n), 1) >> 2) & 1
    upper = ones_where((iota((n, n), 0) < iota((n, n), 1)) & (side_in == side_out))
    rank = dot(live.astype(bf16), upper)
    code = jnp.where(live > 0.5, rank + (side * half).astype(f32), -1.0)
    code_t = code.T
    offsets = [[], []]
    ends = []
    for j in range(2):
        sizes = jnp.sum(jnp.where(side == j, live, 0.0), axis=1, keepdims=True).astype(i32)
        offset = jnp.int32(0)
        for g in range(groups):
            offsets[j].append(pl.multiple_of(offset, 16))
            offset = offset + ((sizes[g, 0] + 15) >> 4) * 16
        ends.append(offset)
    for g in range(groups):
        rows = dot(pick_rows(code[g : g + 1, :], (n, n)), slots(g)).astype(bf16)
        for j in range(2):
            qc_ref[j, pl.ds(offsets[j][g], half), :] = rows[j * half : (j + 1) * half]
    for j in range(2):
        after = pl.multiple_of(offsets[j][groups - 1] + half, 16)
        qc_ref[j, pl.ds(after, QB), :] = jnp.zeros((QB, D), bf16)
    fast = jnp.max(unsafe) < 0.5

    chunks = [(end + QB - 1) // QB for end in ends]
    blocks = [(key_count(j ^ core) + KB - 1) // KB for j in range(2)]

    def pick(j, pair):
        return jnp.where(j == 0, pair[0], pair[1])

    def queries_of(h):
        pieces = [
            qt_ref[h * HD : (h + 1) * HD, :] if k == h % 4 else jnp.zeros((HD, QB), bf16)
            for k in range(4)
        ]
        return jnp.concatenate(pieces, axis=0)

    def keys_of(u, kb, h):
        return k_ref[u, kb, :, (h // 4) * 128 : (h // 4 + 1) * 128]

    def finish(j, start, values, masses):
        count = values.shape[1]
        row = iota((8, count), 0)
        tiles = []
        for hh in range(4):
            low, high = masses(hh), masses(hh + 4)
            tile = jnp.zeros((8, count), f32)
            for k in range(len(low)):
                tile = jnp.where((row & 3) == k, jnp.where(row < 4, low[k], high[k]), tile)
            tiles.append(tile)
        wide = jnp.concatenate([values] + tiles * 4, axis=0).astype(bf16)
        turned = dot_t(ones_where(iota((count, count), 0) == iota((count, count), 1)), wide).astype(bf16)
        oc_ref[j, pl.ds(start, count), :] = turned

    def two(total):
        high = total.astype(bf16).astype(f32)
        return high, total - high

    def weights(u, kb, h):
        p_ref[h] = jnp.exp2(dot(keys_of(u, kb, h), queries_of(h)) * SCALE2).astype(bf16)

    def load_queries(j, ch):
        qt_ref[...] = qc_ref[j, pl.ds(pl.multiple_of(ch * QB, QB), QB), :].T

    def add_values(u, kb, h):
        lhs = jnp.concatenate([vt_ref[u, kb, h * HD : (h + 1) * HD, :], valid_ref[u, kb]], axis=0)
        acc_ref[h] += dot(lhs, p_ref[h])

    def fast_item(index, carry):
        j, ch, kb = carry
        ends_chunk = kb + 1 == pick(j, blocks)
        kb_next = jnp.where(ends_chunk, 0, kb + 1)
        ch_next = jnp.where(ends_chunk, ch + 1, ch)
        ends_bucket = ch_next == pick(j, chunks)
        ch_next = jnp.where(ends_bucket, 0, ch_next)
        j_next = jnp.minimum(jnp.where(ends_bucket, j + 1, j), 1)

        @pl.when(ends_chunk)
        def _():
            load_queries(j_next, ch_next)

        for h in range(0, H, 2):
            add_values(j ^ core, kb, h)
            add_values(j ^ core, kb, h + 1)
            weights(j_next ^ core, kb_next, h)
            weights(j_next ^ core, kb_next, h + 1)

        @pl.when(ends_chunk)
        def _():
            finish(
                j, pl.multiple_of(ch * QB, QB),
                jnp.concatenate([acc_ref[h, 0:HD, :] for h in range(H)], axis=0),
                lambda h: two(acc_ref[h, HD : HD + 8, :]),
            )
            acc_ref[...] = jnp.zeros(acc_ref.shape, f32)

        return j_next, ch_next, kb_next

    def slow_chunk(j, u, start, blocks, keys):
        acc_ref[...] = jnp.zeros(acc_ref.shape, f32)
        max_ref[...] = jnp.full(max_ref.shape, -3e38, f32)
        qt_ref[...] = qc_ref[j, pl.ds(start, QB), :].T

        def scores(kb, h):
            s = dot(keys_of(u, kb, h), queries_of(h)) * SCALE2
            return s, (iota((KB, QB), 0) + kb * KB) < keys

        def find(kb, carry):
            for h in range(H):
                s, valid = scores(kb, h)
                top = jnp.max(jnp.where(valid, s, -3e38), axis=0, keepdims=True)
                max_ref[h] = jnp.maximum(max_ref[h], top)
            return carry

        def block(kb, carry):
            for h in range(H):
                s, valid = scores(kb, h)
                p = jnp.where(valid, jnp.exp2(s - max_ref[h, 0:1, :]), 0.0).astype(bf16)
                lhs = jnp.concatenate([vt_ref[u, kb, h * HD : (h + 1) * HD, :], valid_ref[u, kb]], axis=0)
                acc_ref[h] += dot(lhs, p)
            return carry

        lax.fori_loop(0, blocks, find, 0)
        lax.fori_loop(0, blocks, block, 0)

        def masses(h):
            mass = jnp.log2(acc_ref[h, HD : HD + 8, :]) + max_ref[h]
            top, rest = two(mass)
            rest = rest.astype(bf16).astype(f32)
            return two(jnp.exp2(mass - top - rest)) + (top, rest)

        values = [acc_ref[h, 0:HD, :] / acc_ref[h, HD : HD + 1, :] for h in range(H)]
        finish(j, start, jnp.concatenate(values, axis=0), masses)

    @pl.when(fast)
    def _():
        start = jnp.where(chunks[0] > 0, 0, 1)
        load_queries(start, 0)
        acc_ref[...] = jnp.zeros(acc_ref.shape, f32)
        for h in range(H):
            weights(start ^ core, 0, h)
        total = chunks[0] * blocks[0] + chunks[1] * blocks[1]
        lax.fori_loop(0, total, fast_item, (start, jnp.int32(0), jnp.int32(0)))

    @pl.when(jnp.logical_not(fast))
    def _():
        def bucket(j, carry):
            def chunk(ch, carry):
                slow_chunk(j, j ^ core, pl.multiple_of(ch * QB, QB), pick(j, blocks), key_count(j ^ core))
                return carry

            return lax.fori_loop(0, pick(j, chunks), chunk, carry)

        lax.fori_loop(0, 2, bucket, 0)

    for j in range(2):
        done = pl.multiple_of(chunks[j] * QB, QB)
        oc_ref[j, pl.ds(done, half), :] = jnp.zeros((half, D + 128), bf16)

    own_lanes = (iota((8, 128), 1) >> 5) == (iota((8, 128), 0) & 3)
    own_lanes = jnp.concatenate([jnp.where(own_lanes, 1.0, 0.0)] * (n // 8), axis=0)
    mass_row = iota((8 * srcs, n), 0)
    mass_slot = iota((8 * srcs, n), 1)
    collect = ones_where(mass_row == (mass_slot >> 5) * 8 + ((mass_slot & 31) >> 2))

    def unpack(g):
        scatter = pick_rows(code_t[:, g : g + 1], (n, n))
        packed = jnp.concatenate([oc_ref[j, pl.ds(offsets[j][g], half), :] for j in range(2)], axis=0)
        return dot(scatter, packed)

    def write(g, rows):
        for k in range(2):
            out = rows[:, k * 128 : (k + 1) * 128].astype(bf16)
            ret_ref[srcs * g : srcs * (g + 1), k * SLOTS : (k + 1) * SLOTS, :] = out.reshape(srcs, SLOTS, 128)
        return (rows[:, D:] * own_lanes).astype(bf16)

    ahead = [unpack(g) for g in range(2)]
    spread = []
    for g in range(groups):
        if g + 2 < groups:
            ahead.append(unpack(g + 2))
        spread.append(write(g, ahead[g]))
    for g in range(groups):
        out = dot(collect, spread[g]).astype(bf16)
        ret_ref[srcs * g : srcs * (g + 1), 2 * SLOTS : 2 * SLOTS + 8, :] = out.reshape(srcs, 8, 128)


def combine_kernel(pos_ref, ret_ref, out_hbm, out_ref, out_sem):
    n = 128
    steps = out_ref.shape[0]
    chips = ret_ref.shape[0]
    pos = pos_ref[...].T
    lane_in = iota((n, D), 0) & 31
    head = iota((n, D), 1) // HD
    same_head = (lane_in >> 2) == 2 * (head & 3) + (head >> 2)
    widen = jnp.concatenate(
        [ones_where(same_head & ((lane_in & 3) < 2)), ones_where(same_head & ((lane_in & 3) >= 2))], axis=1
    )
    lane_slot = iota((2 * n, 128), 1) >> 5
    masses = ret_ref[:, 2 * SLOTS : 2 * SLOTS + 8, :].reshape(chips * 8, 128)
    copies = []
    lane = iota((2 * n, 128), 1)

    def gather(t):
        at = jnp.concatenate(
            [jnp.broadcast_to(pos[:, 2 * t + j : 2 * t + j + 1], (n, 128)) for j in range(2)], axis=0
        ).astype(i32)
        chip = at >> 5

        def pick(where):
            return jnp.concatenate([ones_where(lane == where - 128 * k) for k in range(chips * 8 // 128)], axis=1)

        values = pick(chip * 8 + (at & 7))
        values = [
            dot(values, ret_ref[:, k * SLOTS + 8 * t : k * SLOTS + 8 * t + 8, :].reshape(chips * 8, 128))
            for k in range(2)
        ]
        mass = dot(pick(chip * 8 + 2 * t + ((at >> 2) & 1)), masses)
        return jnp.concatenate(values, axis=1), jnp.where(lane_slot == (at & 3), mass, 0.0).astype(bf16)

    def merge(t, values, wide):
        total, top = wide[:, :D], wide[:, D:]
        highest = jnp.maximum(top[:n], top[n:])
        w0 = jnp.exp2(top[:n] - highest)
        w1 = jnp.exp2(top[n:] - highest)
        merged = (w0 * values[:n] + w1 * values[n:]) / (w0 * total[:n] + w1 * total[n:])
        out_ref[t] = merged.astype(bf16)
        copies.append(pltpu.make_async_copy(out_ref.at[t], out_hbm.at[t], out_sem.at[t]))
        copies[-1].start()

    ahead = [gather(0)]
    for t in range(steps):
        if t + 1 < steps:
            ahead.append(gather(t + 1))
        values, mass = ahead[t]
        merge(t, values, dot(mass, widen))
    for copy in copies:
        copy.wait()


def near(x):
    return pltpu.with_memory_space_constraint(x, pltpu.VMEM)


def hbm(x):
    return pltpu.with_memory_space_constraint(x, pltpu.HBM)


def call(kernel, name, mib, outs, args, scratch=()):
    spec = pl.BlockSpec(memory_space=pltpu.VMEM)
    single = not isinstance(outs, tuple)
    return pl.pallas_call(
        kernel,
        out_shape=outs,
        in_specs=[spec] * len(args),
        out_specs=spec if single else tuple(spec for _ in outs),
        scratch_shapes=list(scratch),
        compiler_params=pltpu.CompilerParams(vmem_limit_bytes=mib << 20),
        name=name,
    )(*args)


def body(queries, probes, keys, values, bucket_home, bucket_rows):
    chips = lax.axis_size("y") * lax.axis_size("col")
    steps = queries.shape[0]
    swap = [(0, 1), (1, 0)]
    k_own, v_own = keys[0], values[0]
    k_other = lax.ppermute(k_own, "core", swap)
    v_other = lax.ppermute(v_own, "core", swap)
    home = bucket_home.reshape(1, 128)
    rows = bucket_rows.reshape(1, 128)
    far = pl.BlockSpec(memory_space=pltpu.HBM)
    send, pos = pl.pallas_call(
        dispatch_kernel,
        out_shape=(jax.ShapeDtypeStruct((chips, SLOTS, D), bf16), pltpu.VMEM((2 * steps, 128), f32)),
        in_specs=[far] * 3,
        out_specs=(far, pl.BlockSpec(memory_space=pltpu.VMEM)),
        scratch_shapes=[
            pltpu.VMEM((steps, 2, 128), i32),
            pltpu.VMEM((1, 128), i32),
            pltpu.VMEM(queries.shape, bf16),
            pltpu.VMEM((chips, SLOTS, D), bf16),
            pltpu.SemaphoreType.DMA((3,)),
            pltpu.SemaphoreType.DMA((chips * SLOTS // 256,)),
        ],
        compiler_params=pltpu.CompilerParams(vmem_limit_bytes=16 << 20),
        name="dispatch",
    )(hbm(probes.transpose(0, 2, 1)), hbm(home), hbm(queries))
    recv = lax.all_to_all(send, ("y", "col"), split_axis=0, concat_axis=0, tiled=True)
    k, vt, valid, stat = call(
        prepare_kernel, "prepare", 16,
        (
            pltpu.VMEM((2, 4, KB, D), bf16),
            pltpu.VMEM((2, 4, D, KB), bf16),
            pltpu.VMEM((2, 4, 16, KB), bf16),
            pltpu.VMEM((2, 8, D), f32),
        ),
        (home, rows, hbm(k_own), hbm(v_own), k_other, v_other),
    )
    padded = chips * 16 + QB
    ret = call(
        attention_kernel, "attention", 24,
        pltpu.VMEM((chips, RET, 128), bf16),
        (home, rows, near(recv), near(k), near(vt), near(valid), near(stat)),
        (
            pltpu.VMEM((2, padded, D), bf16),
            pltpu.VMEM((2, padded, D + 128), bf16),
            pltpu.VMEM((D, QB), bf16),
            pltpu.VMEM((H, KB, QB), bf16),
            pltpu.VMEM((H, HD + 16, QB), f32),
            pltpu.VMEM((H, 8, QB), f32),
        ),
    )
    back = lax.all_to_all(ret, ("y", "col"), split_axis=0, concat_axis=0, tiled=True)
    return pl.pallas_call(
        combine_kernel,
        out_shape=jax.ShapeDtypeStruct(queries.shape, bf16),
        in_specs=[pl.BlockSpec(memory_space=pltpu.VMEM)] * 2,
        out_specs=far,
        scratch_shapes=[pltpu.VMEM(queries.shape, bf16), pltpu.SemaphoreType.DMA((steps,))],
        compiler_params=pltpu.CompilerParams(vmem_limit_bytes=24 << 20),
        name="combine",
    )(near(pos), near(back))


def solution(mesh):
    rows, columns = mesh.devices.shape
    split = Mesh(mesh.devices.reshape(rows // 2, 2, columns), ("y", "core", "col"))
    every = ("y", "core", "col")
    return jax.shard_map(
        body,
        mesh=split,
        in_specs=(
            P(None, every, None),
            P(None, every, None),
            P(every, None, None),
            P(every, None, None),
            P(),
            P(),
        ),
        out_specs=P(None, every, None),
        check_vma=False,
    )
```

```python
import math

import jax
import jax.numpy as jnp
from jax import lax
from jax.experimental import pallas as pl
from jax.experimental.pallas import tpu as pltpu
from jax.sharding import Mesh, PartitionSpec as P

H = 8
HD = 32
D = 256
KB = 256
QB = 256
EARLY = 4
SLOTS = 32
RET = 72
SCALE2 = math.log2(math.e) / math.sqrt(HD)
TINY = 2.0**-60
SAFE = 80.0
NORMS = (SAFE / SCALE2) ** 2 / 1.05

f32 = jnp.float32
bf16 = jnp.bfloat16
i32 = jnp.int32


def iota(shape, dim):
    return lax.broadcasted_iota(i32, shape, dim)


def dot(a, b):
    return jnp.dot(a, b, preferred_element_type=f32)


def dot_t(a, b):
    return lax.dot_general(a, b, (((1,), (1,)), ((), ())), preferred_element_type=f32)


def ones_where(cond):
    return jnp.where(cond, 1.0, 0.0).astype(bf16)


def pick_rows(index, shape):
    along = 1 if index.shape[1] == 1 else 0
    grid = iota(shape, along).astype(f32).astype(bf16)
    return jnp.where(grid == index.astype(bf16), jnp.ones(shape, bf16), jnp.zeros(shape, bf16))


def dispatch_kernel(probes_hbm, home_hbm, q_hbm, send_hbm, pos_ref, probes_ref, home_ref, q_ref, send_ref, in_sem, out_sem):
    copies = [
        pltpu.make_async_copy(source, target, in_sem.at[k])
        for k, (source, target) in enumerate(((home_hbm, home_ref), (probes_hbm, probes_ref), (q_hbm, q_ref)))
    ]
    for copy in copies:
        copy.start()
    steps = probes_ref.shape[0]
    n = 128
    tri = jnp.concatenate(
        [ones_where(iota((n, n), 0) < iota((n, n), 1)), jnp.ones((n, n), bf16)], axis=1
    )
    eye = iota((n, n), 0) == iota((n, n), 1)
    bucket = iota((n, n), 0)
    copies[0].wait()
    home_row = jnp.broadcast_to(home_ref[...].astype(f32), (n, n))
    home = dot(jnp.where(eye, home_row, 0.0).astype(bf16), jnp.ones((n, n), bf16)).astype(i32)
    core = (home >> 4) & 1
    chip = ((home >> 5) << 4) + (home & 15)
    base = (chip * 8 + core * 4).astype(f32)
    copies[1].wait()
    hits = [[bucket == probes_ref[t, j : j + 1, :] for j in range(2)] for t in range(steps)]
    counts = [[dot(ones_where(hit), tri) for hit in pair] for pair in hits]
    pos_rows = []
    for t in range(steps):
        before = base
        for j in range(2):
            mine = jnp.where(hits[t][j], counts[t][j][:, :n] + before, 0.0)
            pos_rows.append(jnp.sum(mine, axis=0, keepdims=True))
            before = before + counts[t][j][:, n:]
    pos = jnp.concatenate(pos_rows, axis=0)
    pos_ref[...] = pos
    rows = 256
    chips = rows // 8
    copies[2].wait()
    out_copies = []
    for t in range(steps):
        lead = q_ref[t, :, :n]
        tiny = (iota((n, n), 1) == 0) & (jnp.abs(lead.astype(f32)) < TINY)
        queries = jnp.concatenate([jnp.where(tiny, jnp.full(lead.shape, TINY, bf16), lead), q_ref[t, :, n:]], axis=1)
        for block in range(send_ref.shape[0] // chips):
            pick = sum(pick_rows(pos[2 * t + j : 2 * t + j + 1] - block * rows, (rows, n)) for j in range(2))
            out = dot(pick, queries).astype(bf16)
            send_ref[block * chips : (block + 1) * chips, 8 * t : 8 * t + 8, :] = out.reshape(chips, 8, D)
        part = pl.ds(8 * t, 8)
        out_copies.append(pltpu.make_async_copy(send_ref.at[:, part, :], send_hbm.at[:, part, :], out_sem.at[t]))
        out_copies[-1].start()
    for copy in out_copies:
        copy.wait()


def bucket_sizes(home_ref, rows_ref):
    core = lax.axis_index("core")
    columns = lax.axis_size("col")
    device = (lax.axis_index("y") * 2 + core) * columns + lax.axis_index("col")
    partner = device + columns * (1 - 2 * core)
    rows = rows_ref[...].astype(f32)

    def size(where):
        return jnp.sum(jnp.where(home_ref[...] == where, rows, 0.0)).astype(i32)

    return core, size(device), size(partner)


def prepare_kernel(home_ref, rows_ref, k_own, v_own, k_other, v_other, k_ref, vt_ref, valid_ref, stat_ref):
    _, own, other = bucket_sizes(home_ref, rows_ref)
    head_sum = ones_where((iota((D, 128), 0) // HD) == iota((D, 128), 1))
    for u in range(2):
        key_ref = (k_own, k_other)[u]
        value_ref = (v_own, v_other)[u]
        count = (own, other)[u]
        norm = jnp.zeros((KB, 128), f32)
        for kb in range(1024 // KB):
            key = key_ref[kb * KB : (kb + 1) * KB, :]
            k_ref[u, kb] = key
            norm = jnp.maximum(norm, dot(key * key, head_sum))
            valid = ones_where((iota((16, KB), 1) + kb * KB) < count)
            valid_ref[u, kb] = valid
            value = value_ref[kb * KB : (kb + 1) * KB, :]
            vt_ref[u, kb] = value.T * valid[0:1, :]
        stat_ref[u] = jnp.full((8, D), jnp.max(norm), f32)


def attention_kernel(
    home_ref, rows_ref, recv_ref, k_ref, vt_ref, valid_ref, stat_ref, ret_ref,
    qc_ref, oc_ref, qt_ref, late_ref, p_ref, acc_ref, max_ref,
):
    n = 256
    half = n // 2
    srcs = n // SLOTS
    groups = recv_ref.shape[0] // srcs
    core, own, other = bucket_sizes(home_ref, rows_ref)

    def key_count(u):
        return jnp.where(u == 0, own, other)

    def slots(g):
        return recv_ref[srcs * g : srcs * (g + 1)].reshape(n, D)

    row = iota((groups, n), 0)
    side = (iota((1, n), 1) >> 2) & 1
    heads = ones_where((iota((16, D), 1) // HD) == iota((16, D), 0))
    norm = jnp.zeros((groups, n), f32)
    unsafe = jnp.zeros((8, n), f32)
    keys_norm = jnp.maximum(stat_ref[0, 0:1, :], stat_ref[1, 0:1, :])
    for g in range(groups):
        q = slots(g)
        squares = dot_t(heads, q * q)[0:8, :]
        unsafe = jnp.maximum(unsafe, jnp.where(squares * keys_norm <= NORMS, 0.0, 1.0))
        norm = jnp.where(row == g, jnp.sum(squares, axis=0, keepdims=True), norm)
    live = jnp.where(norm <= 0.0, 0.0, 1.0)
    side_in = (iota((n, n), 0) >> 2) & 1
    side_out = (iota((n, n), 1) >> 2) & 1
    upper = ones_where((iota((n, n), 0) < iota((n, n), 1)) & (side_in == side_out))
    rank = dot(live.astype(bf16), upper)
    code = jnp.where(live > 0.5, rank + (side * half).astype(f32), -1.0)
    code_t = code.T
    offsets = [[], []]
    ends = []
    for j in range(2):
        sizes = jnp.sum(jnp.where(side == j, live, 0.0), axis=1, keepdims=True).astype(i32)
        offset = jnp.int32(0)
        for g in range(groups):
            offsets[j].append(pl.multiple_of(offset, 16))
            offset = offset + ((sizes[g, 0] + 15) >> 4) * 16
        ends.append(offset)
    for g in range(groups):
        rows = dot(pick_rows(code[g : g + 1, :], (n, n)), slots(g)).astype(bf16)
        for j in range(2):
            qc_ref[j, pl.ds(offsets[j][g], half), :] = rows[j * half : (j + 1) * half]
    for j in range(2):
        after = pl.multiple_of(offsets[j][groups - 1] + half, 16)
        qc_ref[j, pl.ds(after, QB), :] = jnp.zeros((QB, D), bf16)
    fast = jnp.max(unsafe) < 0.5

    chunks = [(end + QB - 1) // QB for end in ends]
    blocks = [(key_count(j ^ core) + KB - 1) // KB for j in range(2)]

    def pick(j, pair):
        return jnp.where(j == 0, pair[0], pair[1])

    def queries_of(h):
        pieces = [
            qt_ref[h * HD : (h + 1) * HD, :] if k == h % 4 else jnp.zeros((HD, QB), bf16)
            for k in range(4)
        ]
        return jnp.concatenate(pieces, axis=0)

    def keys_of(u, kb, h):
        return k_ref[u, kb, :, (h // 4) * 128 : (h // 4 + 1) * 128]

    def finish(j, start, values, masses):
        count = values.shape[1]
        row = iota((8, count), 0)
        tiles = []
        for hh in range(4):
            low, high = masses(hh), masses(hh + 4)
            tile = jnp.zeros((8, count), f32)
            for k in range(len(low)):
                tile = jnp.where((row & 3) == k, jnp.where(row < 4, low[k], high[k]), tile)
            tiles.append(tile)
        wide = jnp.concatenate([values] + tiles * 4, axis=0).astype(bf16)
        turned = dot_t(ones_where(iota((count, count), 0) == iota((count, count), 1)), wide).astype(bf16)
        oc_ref[j, pl.ds(start, count), :] = turned

    def two(total):
        high = total.astype(bf16).astype(f32)
        return high, total - high

    def weights(u, kb, h, queries):
        p_ref[h] = jnp.exp2(dot(keys_of(u, kb, h), queries) * SCALE2).astype(bf16)

    def late_queries_of(h):
        part = late_ref[(h - EARLY) * HD : (h - EARLY + 1) * HD, :]
        return jnp.concatenate([part if k == h % 4 else jnp.zeros((HD, QB), bf16) for k in range(4)], axis=0)

    def load_queries(j, ch):
        qt_ref[...] = qc_ref[j, pl.ds(pl.multiple_of(ch * QB, QB), QB), :].T

    def add_values(u, kb, h):
        lhs = jnp.concatenate([vt_ref[u, kb, h * HD : (h + 1) * HD, :], valid_ref[u, kb]], axis=0)
        acc_ref[h] += dot(lhs, p_ref[h])

    def fast_item(index, carry):
        j, ch, kb = carry
        ends_chunk = kb + 1 == pick(j, blocks)
        kb_next = jnp.where(ends_chunk, 0, kb + 1)
        ch_next = jnp.where(ends_chunk, ch + 1, ch)
        ends_bucket = ch_next == pick(j, chunks)
        ch_next = jnp.where(ends_bucket, 0, ch_next)
        j_next = jnp.minimum(jnp.where(ends_bucket, j + 1, j), 1)

        @pl.when(kb == 0)
        def _():
            late_ref[...] = qt_ref[EARLY * HD :, :]

        @pl.when(ends_chunk)
        def _():
            load_queries(j_next, ch_next)

        u, u_next = j ^ core, j_next ^ core
        for h in range(EARLY, H):
            weights(u, kb, h, late_queries_of(h))
        add_values(u, kb, 0)
        add_values(u, kb, 1)
        for h in range(EARLY):
            weights(u_next, kb_next, h, queries_of(h))
            if h + 2 < EARLY:
                add_values(u, kb, h + 2)
        for h in range(EARLY, H):
            add_values(u, kb, h)

        @pl.when(ends_chunk)
        def _():
            finish(
                j, pl.multiple_of(ch * QB, QB),
                jnp.concatenate([acc_ref[h, 0:HD, :] for h in range(H)], axis=0),
                lambda h: two(acc_ref[h, HD : HD + 8, :]),
            )
            acc_ref[...] = jnp.zeros(acc_ref.shape, f32)

        return j_next, ch_next, kb_next

    def slow_chunk(j, u, start, blocks, keys):
        acc_ref[...] = jnp.zeros(acc_ref.shape, f32)
        max_ref[...] = jnp.full(max_ref.shape, -3e38, f32)
        qt_ref[...] = qc_ref[j, pl.ds(start, QB), :].T

        def scores(kb, h):
            s = dot(keys_of(u, kb, h), queries_of(h)) * SCALE2
            return s, (iota((KB, QB), 0) + kb * KB) < keys

        def find(kb, carry):
            for h in range(H):
                s, valid = scores(kb, h)
                top = jnp.max(jnp.where(valid, s, -3e38), axis=0, keepdims=True)
                max_ref[h] = jnp.maximum(max_ref[h], top)
            return carry

        def block(kb, carry):
            for h in range(H):
                s, valid = scores(kb, h)
                p = jnp.where(valid, jnp.exp2(s - max_ref[h, 0:1, :]), 0.0).astype(bf16)
                lhs = jnp.concatenate([vt_ref[u, kb, h * HD : (h + 1) * HD, :], valid_ref[u, kb]], axis=0)
                acc_ref[h] += dot(lhs, p)
            return carry

        lax.fori_loop(0, blocks, find, 0)
        lax.fori_loop(0, blocks, block, 0)

        def masses(h):
            mass = jnp.log2(acc_ref[h, HD : HD + 8, :]) + max_ref[h]
            top, rest = two(mass)
            rest = rest.astype(bf16).astype(f32)
            return two(jnp.exp2(mass - top - rest)) + (top, rest)

        values = [acc_ref[h, 0:HD, :] / acc_ref[h, HD : HD + 1, :] for h in range(H)]
        finish(j, start, jnp.concatenate(values, axis=0), masses)

    @pl.when(fast)
    def _():
        start = jnp.where(chunks[0] > 0, 0, 1)
        load_queries(start, 0)
        acc_ref[...] = jnp.zeros(acc_ref.shape, f32)
        for h in range(EARLY):
            weights(start ^ core, 0, h, queries_of(h))
        total = chunks[0] * blocks[0] + chunks[1] * blocks[1]
        lax.fori_loop(0, total, fast_item, (start, jnp.int32(0), jnp.int32(0)))

    @pl.when(jnp.logical_not(fast))
    def _():
        def bucket(j, carry):
            def chunk(ch, carry):
                slow_chunk(j, j ^ core, pl.multiple_of(ch * QB, QB), pick(j, blocks), key_count(j ^ core))
                return carry

            return lax.fori_loop(0, pick(j, chunks), chunk, carry)

        lax.fori_loop(0, 2, bucket, 0)

    for j in range(2):
        done = pl.multiple_of(chunks[j] * QB, QB)
        oc_ref[j, pl.ds(done, half), :] = jnp.zeros((half, D + 128), bf16)

    own_lanes = (iota((8, 128), 1) >> 5) == (iota((8, 128), 0) & 3)
    own_lanes = jnp.concatenate([jnp.where(own_lanes, 1.0, 0.0)] * (n // 8), axis=0)
    mass_row = iota((8 * srcs, n), 0)
    mass_slot = iota((8 * srcs, n), 1)
    collect = ones_where(mass_row == (mass_slot >> 5) * 8 + ((mass_slot & 31) >> 2))

    def unpack(g):
        scatter = pick_rows(code_t[:, g : g + 1], (n, n))
        packed = jnp.concatenate([oc_ref[j, pl.ds(offsets[j][g], half), :] for j in range(2)], axis=0)
        return dot(scatter, packed)

    def write(g, rows):
        for k in range(2):
            out = rows[:, k * 128 : (k + 1) * 128].astype(bf16)
            ret_ref[srcs * g : srcs * (g + 1), k * SLOTS : (k + 1) * SLOTS, :] = out.reshape(srcs, SLOTS, 128)
        return (rows[:, D:] * own_lanes).astype(bf16)

    ahead = [unpack(g) for g in range(2)]
    spread = []
    for g in range(groups):
        if g + 2 < groups:
            ahead.append(unpack(g + 2))
        spread.append(write(g, ahead[g]))
    for g in range(groups):
        out = dot(collect, spread[g]).astype(bf16)
        ret_ref[srcs * g : srcs * (g + 1), 2 * SLOTS : 2 * SLOTS + 8, :] = out.reshape(srcs, 8, 128)


def combine_kernel(pos_ref, ret_ref, out_hbm, out_ref, out_sem):
    n = 128
    steps = out_ref.shape[0]
    chips = ret_ref.shape[0]
    lane_in = iota((n, D), 0) & 31
    head = iota((n, D), 1) // HD
    same_head = (lane_in >> 2) == 2 * (head & 3) + (head >> 2)
    widen = jnp.concatenate(
        [ones_where(same_head & ((lane_in & 3) < 2)), ones_where(same_head & ((lane_in & 3) >= 2))], axis=1
    )
    at = pos_ref[...].astype(i32)
    step = iota(at.shape, 0) >> 1
    columns = []
    for row in (at, (at & -8) + 2 * step + ((at >> 2) & 1)):
        columns += [jnp.where(row < 256, row, -1), jnp.where(row < 256, -1, row - 256)]
    columns = jnp.concatenate(columns + [at & 3], axis=0).astype(f32).T
    lane_slot = (iota((2 * n, n), 1) >> 5).astype(f32).astype(bf16)
    lanes = [(iota((2 * n, n), 1) + n * k).astype(f32).astype(bf16) for k in range(2)]
    one, zero = jnp.ones((2 * n, n), bf16), jnp.zeros((2 * n, n), bf16)
    masses = ret_ref[:, 2 * SLOTS : 2 * SLOTS + 8, :].reshape(chips * 8, 128)
    copies = []

    def gather(t):
        def column(k):
            first = 8 * k + 2 * t
            both = [jnp.broadcast_to(columns[:, c : c + 1], (n, n)) for c in (first, first + 1)]
            return jnp.concatenate(both, axis=0).astype(bf16)

        def pick(k):
            return jnp.concatenate(
                [jnp.where(column(k + side) == lane, one, zero) for side in range(2) for lane in lanes], axis=1
            )

        rows = [ret_ref[:, k * SLOTS + 8 * t : k * SLOTS + 8 * t + 8, :].reshape(chips * 8, 128) for k in range(2)]
        values = dot(pick(0), jnp.concatenate(rows, axis=1))
        mass = dot(pick(2), masses).astype(bf16)
        return values, jnp.where(column(4) == lane_slot, mass, zero)

    def merge(t, values, wide):
        total, top = wide[:, :D], wide[:, D:]
        highest = jnp.maximum(top[:n], top[n:])
        w0 = jnp.exp2(top[:n] - highest)
        w1 = jnp.exp2(top[n:] - highest)
        merged = (w0 * values[:n] + w1 * values[n:]) / (w0 * total[:n] + w1 * total[n:])
        out_ref[t] = merged.astype(bf16)
        copies.append(pltpu.make_async_copy(out_ref.at[t], out_hbm.at[t], out_sem.at[t]))
        copies[-1].start()

    ahead = [gather(0)]
    for t in range(steps):
        if t + 1 < steps:
            ahead.append(gather(t + 1))
        values, mass = ahead[t]
        merge(t, values, dot(mass, widen))
    for copy in copies:
        copy.wait()


def near(x):
    return pltpu.with_memory_space_constraint(x, pltpu.VMEM)


def hbm(x):
    return pltpu.with_memory_space_constraint(x, pltpu.HBM)


def call(kernel, name, mib, outs, args, scratch=()):
    spec = pl.BlockSpec(memory_space=pltpu.VMEM)
    single = not isinstance(outs, tuple)
    return pl.pallas_call(
        kernel,
        out_shape=outs,
        in_specs=[spec] * len(args),
        out_specs=spec if single else tuple(spec for _ in outs),
        scratch_shapes=list(scratch),
        compiler_params=pltpu.CompilerParams(vmem_limit_bytes=mib << 20),
        name=name,
    )(*args)


def body(queries, probes, keys, values, bucket_home, bucket_rows):
    chips = lax.axis_size("y") * lax.axis_size("col")
    steps = queries.shape[0]
    swap = [(0, 1), (1, 0)]
    k_own, v_own = keys[0], values[0]
    k_other = lax.ppermute(k_own, "core", swap)
    v_other = lax.ppermute(v_own, "core", swap)
    home = bucket_home.reshape(1, 128)
    rows = bucket_rows.reshape(1, 128)
    far = pl.BlockSpec(memory_space=pltpu.HBM)
    send, pos = pl.pallas_call(
        dispatch_kernel,
        out_shape=(jax.ShapeDtypeStruct((chips, SLOTS, D), bf16), pltpu.VMEM((2 * steps, 128), f32)),
        in_specs=[far] * 3,
        out_specs=(far, pl.BlockSpec(memory_space=pltpu.VMEM)),
        scratch_shapes=[
            pltpu.VMEM((steps, 2, 128), i32),
            pltpu.VMEM((1, 128), i32),
            pltpu.VMEM(queries.shape, bf16),
            pltpu.VMEM((chips, SLOTS, D), bf16),
            pltpu.SemaphoreType.DMA((3,)),
            pltpu.SemaphoreType.DMA((steps,)),
        ],
        compiler_params=pltpu.CompilerParams(vmem_limit_bytes=16 << 20),
        name="dispatch",
    )(hbm(probes.transpose(0, 2, 1)), hbm(home), hbm(queries))
    recv = lax.all_to_all(send, ("y", "col"), split_axis=0, concat_axis=0, tiled=True)
    k, vt, valid, stat = call(
        prepare_kernel, "prepare", 16,
        (
            pltpu.VMEM((2, 4, KB, D), bf16),
            pltpu.VMEM((2, 4, D, KB), bf16),
            pltpu.VMEM((2, 4, 16, KB), bf16),
            pltpu.VMEM((2, 8, D), f32),
        ),
        (home, rows, hbm(k_own), hbm(v_own), k_other, v_other),
    )
    padded = chips * 16 + QB
    ret = call(
        attention_kernel, "attention", 24,
        pltpu.VMEM((chips, RET, 128), bf16),
        (home, rows, near(recv), near(k), near(vt), near(valid), near(stat)),
        (
            pltpu.VMEM((2, padded, D), bf16),
            pltpu.VMEM((2, padded, D + 128), bf16),
            pltpu.VMEM((D, QB), bf16),
            pltpu.VMEM(((H - EARLY) * HD, QB), bf16),
            pltpu.VMEM((H, KB, QB), bf16),
            pltpu.VMEM((H, HD + 16, QB), f32),
            pltpu.VMEM((H, 8, QB), f32),
        ),
    )
    back = lax.all_to_all(ret, ("y", "col"), split_axis=0, concat_axis=0, tiled=True)
    return pl.pallas_call(
        combine_kernel,
        out_shape=jax.ShapeDtypeStruct(queries.shape, bf16),
        in_specs=[pl.BlockSpec(memory_space=pltpu.VMEM)] * 2,
        out_specs=far,
        scratch_shapes=[pltpu.VMEM(queries.shape, bf16), pltpu.SemaphoreType.DMA((steps,))],
        compiler_params=pltpu.CompilerParams(vmem_limit_bytes=24 << 20),
        name="combine",
    )(near(pos), near(back))


def solution(mesh):
    rows, columns = mesh.devices.shape
    split = Mesh(mesh.devices.reshape(rows // 2, 2, columns), ("y", "core", "col"))
    every = ("y", "core", "col")
    return jax.shard_map(
        body,
        mesh=split,
        in_specs=(
            P(None, every, None),
            P(None, every, None),
            P(every, None, None),
            P(every, None, None),
            P(),
            P(),
        ),
        out_specs=P(None, every, None),
        check_vma=False,
    )
```

```python
import math

import jax
import jax.numpy as jnp
from jax import lax
from jax.experimental import pallas as pl
from jax.experimental.pallas import tpu as pltpu
from jax.sharding import Mesh, PartitionSpec as P

H = 8
HD = 32
D = 256
KB = 256
QB = 256
EARLY = 4
SLOTS = 32
RET = 72
SCALE2 = math.log2(math.e) / math.sqrt(HD)
TINY = 2.0**-60
SAFE = 80.0
NORMS = (SAFE / SCALE2) ** 2 / 1.05

f32 = jnp.float32
bf16 = jnp.bfloat16
i32 = jnp.int32


def iota(shape, dim):
    return lax.broadcasted_iota(i32, shape, dim)


def dot(a, b):
    return jnp.dot(a, b, preferred_element_type=f32)


def dot_t(a, b):
    return lax.dot_general(a, b, (((1,), (1,)), ((), ())), preferred_element_type=f32)


def ones_where(cond):
    return jnp.where(cond, 1.0, 0.0).astype(bf16)


def pick_rows(index, shape):
    along = 1 if index.shape[1] == 1 else 0
    grid = iota(shape, along).astype(f32).astype(bf16)
    return jnp.where(grid == index.astype(bf16), jnp.ones(shape, bf16), jnp.zeros(shape, bf16))


def dispatch_kernel(probes_hbm, home_hbm, q_hbm, send_hbm, pos_ref, probes_ref, home_ref, q_ref, send_ref, in_sem, out_sem):
    copies = [
        pltpu.make_async_copy(source, target, in_sem.at[k])
        for k, (source, target) in enumerate(((home_hbm, home_ref), (probes_hbm, probes_ref), (q_hbm, q_ref)))
    ]
    for copy in copies:
        copy.start()
    steps = probes_ref.shape[0]
    n = 128
    tri = jnp.concatenate(
        [ones_where(iota((n, n), 0) < iota((n, n), 1)), jnp.ones((n, n), bf16)], axis=1
    )
    eye = iota((n, n), 0) == iota((n, n), 1)
    bucket = iota((n, n), 0)
    copies[0].wait()
    home_row = jnp.broadcast_to(home_ref[...].astype(f32), (n, n))
    home = dot(jnp.where(eye, home_row, 0.0).astype(bf16), jnp.ones((n, n), bf16)).astype(i32)
    core = (home >> 4) & 1
    chip = ((home >> 5) << 4) + (home & 15)
    base = (chip * 8 + core * 4).astype(f32)
    copies[1].wait()
    hits = [[bucket == probes_ref[t, j : j + 1, :] for j in range(2)] for t in range(steps)]
    counts = [[dot(ones_where(hit), tri) for hit in pair] for pair in hits]
    pos_rows = []
    for t in range(steps):
        before = base
        for j in range(2):
            mine = jnp.where(hits[t][j], counts[t][j][:, :n] + before, 0.0)
            pos_rows.append(jnp.sum(mine, axis=0, keepdims=True))
            before = before + counts[t][j][:, n:]
    pos = jnp.concatenate(pos_rows, axis=0)
    pos_ref[...] = pos
    rows = 256
    chips = rows // 8
    copies[2].wait()
    out_copies = []
    for t in range(steps):
        lead = q_ref[t, :, :n]
        tiny = (iota((n, n), 1) == 0) & (jnp.abs(lead.astype(f32)) < TINY)
        queries = jnp.concatenate([jnp.where(tiny, jnp.full(lead.shape, TINY, bf16), lead), q_ref[t, :, n:]], axis=1)
        for block in range(send_ref.shape[0] // chips):
            pick = sum(pick_rows(pos[2 * t + j : 2 * t + j + 1] - block * rows, (rows, n)) for j in range(2))
            out = dot(pick, queries).astype(bf16)
            send_ref[block * chips : (block + 1) * chips, 8 * t : 8 * t + 8, :] = out.reshape(chips, 8, D)
        part = pl.ds(8 * t, 8)
        out_copies.append(pltpu.make_async_copy(send_ref.at[:, part, :], send_hbm.at[:, part, :], out_sem.at[t]))
        out_copies[-1].start()
    for copy in out_copies:
        copy.wait()


def bucket_sizes(home_ref, rows_ref):
    core = lax.axis_index("core")
    columns = lax.axis_size("col")
    device = (lax.axis_index("y") * 2 + core) * columns + lax.axis_index("col")
    partner = device + columns * (1 - 2 * core)
    rows = rows_ref[...].astype(f32)

    def size(where):
        return jnp.sum(jnp.where(home_ref[...] == where, rows, 0.0)).astype(i32)

    return core, size(device), size(partner)


def prepare_kernel(home_ref, rows_ref, k_own, v_own, k_other, v_other, k_ref, vt_ref, valid_ref, stat_ref):
    _, own, other = bucket_sizes(home_ref, rows_ref)
    head_sum = ones_where((iota((D, 128), 0) // HD) == iota((D, 128), 1))
    for u in range(2):
        key_ref = (k_own, k_other)[u]
        value_ref = (v_own, v_other)[u]
        count = (own, other)[u]
        norm = jnp.zeros((KB, 128), f32)
        for kb in range(1024 // KB):
            key = key_ref[kb * KB : (kb + 1) * KB, :]
            k_ref[u, kb] = key
            norm = jnp.maximum(norm, dot(key * key, head_sum))
            valid = ones_where((iota((16, KB), 1) + kb * KB) < count)
            valid_ref[u, kb] = valid
            value = value_ref[kb * KB : (kb + 1) * KB, :]
            vt_ref[u, kb] = value.T * valid[0:1, :]
        stat_ref[u] = jnp.full((8, D), jnp.max(norm), f32)


def attention_kernel(
    home_ref, rows_ref, recv_ref, k_ref, vt_ref, valid_ref, stat_ref, ret_ref,
    qc_ref, oc_ref, qt_ref, late_ref, p_ref, acc_ref, max_ref,
):
    n = 256
    half = n // 2
    srcs = n // SLOTS
    groups = recv_ref.shape[0] // srcs
    core, own, other = bucket_sizes(home_ref, rows_ref)

    def key_count(u):
        return jnp.where(u == 0, own, other)

    def slots(g):
        return recv_ref[srcs * g : srcs * (g + 1)].reshape(n, D)

    row = iota((groups, n), 0)
    side = (iota((1, n), 1) >> 2) & 1
    heads = ones_where((iota((16, D), 1) // HD) == iota((16, D), 0))
    norm = jnp.zeros((groups, n), f32)
    unsafe = jnp.zeros((8, n), f32)
    keys_norm = jnp.maximum(stat_ref[0, 0:1, :], stat_ref[1, 0:1, :])
    for g in range(groups):
        q = slots(g)
        squares = dot_t(heads, q * q)[0:8, :]
        unsafe = jnp.maximum(unsafe, jnp.where(squares * keys_norm <= NORMS, 0.0, 1.0))
        norm = jnp.where(row == g, jnp.sum(squares, axis=0, keepdims=True), norm)
    live = jnp.where(norm <= 0.0, 0.0, 1.0)
    side_in = (iota((n, n), 0) >> 2) & 1
    side_out = (iota((n, n), 1) >> 2) & 1
    upper = ones_where((iota((n, n), 0) < iota((n, n), 1)) & (side_in == side_out))
    rank = dot(live.astype(bf16), upper)
    code = jnp.where(live > 0.5, rank + (side * half).astype(f32), -1.0)
    code_t = code.T
    offsets = [[], []]
    ends = []
    for j in range(2):
        sizes = jnp.sum(jnp.where(side == j, live, 0.0), axis=1, keepdims=True).astype(i32)
        offset = jnp.int32(0)
        for g in range(groups):
            offsets[j].append(pl.multiple_of(offset, 16))
            offset = offset + ((sizes[g, 0] + 15) >> 4) * 16
        ends.append(offset)
    for g in range(groups):
        rows = dot(pick_rows(code[g : g + 1, :], (n, n)), slots(g)).astype(bf16)
        for j in range(2):
            qc_ref[j, pl.ds(offsets[j][g], half), :] = rows[j * half : (j + 1) * half]
    for j in range(2):
        after = pl.multiple_of(offsets[j][groups - 1] + half, 16)
        qc_ref[j, pl.ds(after, QB), :] = jnp.zeros((QB, D), bf16)
    fast = jnp.max(unsafe) < 0.5

    chunks = [(end + QB - 1) // QB for end in ends]
    blocks = [(key_count(j ^ core) + KB - 1) // KB for j in range(2)]

    def pick(j, pair):
        return jnp.where(j == 0, pair[0], pair[1])

    def queries_of(h):
        pieces = [
            qt_ref[h * HD : (h + 1) * HD, :] if k == h % 4 else jnp.zeros((HD, QB), bf16)
            for k in range(4)
        ]
        return jnp.concatenate(pieces, axis=0)

    def keys_of(u, kb, h):
        return k_ref[u, kb, :, (h // 4) * 128 : (h // 4 + 1) * 128]

    def finish(j, start, values, masses):
        count = values.shape[1]
        row = iota((8, count), 0)
        tiles = []
        for hh in range(4):
            low, high = masses(hh), masses(hh + 4)
            tile = jnp.zeros((8, count), f32)
            for k in range(len(low)):
                tile = jnp.where((row & 3) == k, jnp.where(row < 4, low[k], high[k]), tile)
            tiles.append(tile)
        wide = jnp.concatenate([values] + tiles * 4, axis=0).astype(bf16)
        oc_ref[j, pl.ds(start, count), :] = wide.T

    def two(total):
        high = total.astype(bf16).astype(f32)
        return high, total - high

    def weights(u, kb, h, queries):
        p_ref[h] = jnp.exp2(dot(keys_of(u, kb, h), queries) * SCALE2).astype(bf16)

    def late_queries_of(h):
        part = late_ref[(h - EARLY) * HD : (h - EARLY + 1) * HD, :]
        return jnp.concatenate([part if k == h % 4 else jnp.zeros((HD, QB), bf16) for k in range(4)], axis=0)

    def load_queries(j, ch):
        qt_ref[...] = qc_ref[j, pl.ds(pl.multiple_of(ch * QB, QB), QB), :].T

    def add_values(u, kb, h, keep):
        lhs = jnp.concatenate([vt_ref[u, kb, h * HD : (h + 1) * HD, :], valid_ref[u, kb]], axis=0)
        acc_ref[h] = acc_ref[h] * keep + dot(lhs, p_ref[h])

    def fast_item(index, carry):
        j, ch, kb = carry
        ends_chunk = kb + 1 == pick(j, blocks)
        kb_next = jnp.where(ends_chunk, 0, kb + 1)
        ch_next = jnp.where(ends_chunk, ch + 1, ch)
        ends_bucket = ch_next == pick(j, chunks)
        ch_next = jnp.where(ends_bucket, 0, ch_next)
        j_next = jnp.minimum(jnp.where(ends_bucket, j + 1, j), 1)

        @pl.when(kb == 0)
        def _():
            late_ref[...] = qt_ref[EARLY * HD :, :]

        @pl.when(ends_chunk)
        def _():
            load_queries(j_next, ch_next)

        u, u_next = j ^ core, j_next ^ core
        keep = jnp.where(kb == 0, 0.0, 1.0)
        for h in range(EARLY, H):
            weights(u, kb, h, late_queries_of(h))
        add_values(u, kb, 0, keep)
        add_values(u, kb, 1, keep)
        for h in range(EARLY):
            weights(u_next, kb_next, h, queries_of(h))
            if h + 2 < EARLY:
                add_values(u, kb, h + 2, keep)
        for h in range(EARLY, H):
            add_values(u, kb, h, keep)

        @pl.when(ends_chunk)
        def _():
            finish(
                j, pl.multiple_of(ch * QB, QB),
                jnp.concatenate([acc_ref[h, 0:HD, :] for h in range(H)], axis=0),
                lambda h: two(acc_ref[h, HD : HD + 8, :]),
            )

        return j_next, ch_next, kb_next

    def slow_chunk(j, u, start, blocks, keys):
        acc_ref[...] = jnp.zeros(acc_ref.shape, f32)
        max_ref[...] = jnp.full(max_ref.shape, -3e38, f32)
        qt_ref[...] = qc_ref[j, pl.ds(start, QB), :].T

        def scores(kb, h):
            s = dot(keys_of(u, kb, h), queries_of(h)) * SCALE2
            return s, (iota((KB, QB), 0) + kb * KB) < keys

        def find(kb, carry):
            for h in range(H):
                s, valid = scores(kb, h)
                top = jnp.max(jnp.where(valid, s, -3e38), axis=0, keepdims=True)
                max_ref[h] = jnp.maximum(max_ref[h], top)
            return carry

        def block(kb, carry):
            for h in range(H):
                s, valid = scores(kb, h)
                p = jnp.where(valid, jnp.exp2(s - max_ref[h, 0:1, :]), 0.0).astype(bf16)
                lhs = jnp.concatenate([vt_ref[u, kb, h * HD : (h + 1) * HD, :], valid_ref[u, kb]], axis=0)
                acc_ref[h] += dot(lhs, p)
            return carry

        lax.fori_loop(0, blocks, find, 0)
        lax.fori_loop(0, blocks, block, 0)

        def masses(h):
            mass = jnp.log2(acc_ref[h, HD : HD + 8, :]) + max_ref[h]
            top, rest = two(mass)
            rest = rest.astype(bf16).astype(f32)
            return two(jnp.exp2(mass - top - rest)) + (top, rest)

        values = [acc_ref[h, 0:HD, :] / acc_ref[h, HD : HD + 1, :] for h in range(H)]
        finish(j, start, jnp.concatenate(values, axis=0), masses)

    @pl.when(fast)
    def _():
        start = jnp.where(chunks[0] > 0, 0, 1)
        load_queries(start, 0)
        acc_ref[...] = jnp.zeros(acc_ref.shape, f32)
        for h in range(EARLY):
            weights(start ^ core, 0, h, queries_of(h))
        total = chunks[0] * blocks[0] + chunks[1] * blocks[1]
        lax.fori_loop(0, total, fast_item, (start, jnp.int32(0), jnp.int32(0)))

    @pl.when(jnp.logical_not(fast))
    def _():
        def bucket(j, carry):
            def chunk(ch, carry):
                slow_chunk(j, j ^ core, pl.multiple_of(ch * QB, QB), pick(j, blocks), key_count(j ^ core))
                return carry

            return lax.fori_loop(0, pick(j, chunks), chunk, carry)

        lax.fori_loop(0, 2, bucket, 0)

    for j in range(2):
        done = pl.multiple_of(chunks[j] * QB, QB)
        oc_ref[j, pl.ds(done, half), :] = jnp.zeros((half, D + 128), bf16)

    own_lanes = (iota((8, 128), 1) >> 5) == (iota((8, 128), 0) & 3)
    own_lanes = jnp.concatenate([jnp.where(own_lanes, 1.0, 0.0)] * (n // 8), axis=0)
    mass_row = iota((8 * srcs, n), 0)
    mass_slot = iota((8 * srcs, n), 1)
    collect = ones_where(mass_row == (mass_slot >> 5) * 8 + ((mass_slot & 31) >> 2))

    def unpack(g):
        scatter = pick_rows(code_t[:, g : g + 1], (n, n))
        packed = jnp.concatenate([oc_ref[j, pl.ds(offsets[j][g], half), :] for j in range(2)], axis=0)
        return dot(scatter, packed)

    def write(g, rows):
        for k in range(2):
            out = rows[:, k * 128 : (k + 1) * 128].astype(bf16)
            ret_ref[srcs * g : srcs * (g + 1), k * SLOTS : (k + 1) * SLOTS, :] = out.reshape(srcs, SLOTS, 128)
        return (rows[:, D:] * own_lanes).astype(bf16)

    ahead = [unpack(g) for g in range(2)]
    spread = []
    for g in range(groups):
        if g + 2 < groups:
            ahead.append(unpack(g + 2))
        spread.append(write(g, ahead[g]))
    for g in range(groups):
        out = dot(collect, spread[g]).astype(bf16)
        ret_ref[srcs * g : srcs * (g + 1), 2 * SLOTS : 2 * SLOTS + 8, :] = out.reshape(srcs, 8, 128)


def combine_kernel(pos_ref, ret_ref, out_hbm, out_ref, out_sem):
    n = 128
    steps = out_ref.shape[0]
    chips = ret_ref.shape[0]
    lane_in = iota((n, D), 0) & 31
    head = iota((n, D), 1) // HD
    same_head = (lane_in >> 2) == 2 * (head & 3) + (head >> 2)
    widen = jnp.concatenate(
        [ones_where(same_head & ((lane_in & 3) < 2)), ones_where(same_head & ((lane_in & 3) >= 2))], axis=1
    )
    at = pos_ref[...].astype(i32)
    step = iota(at.shape, 0) >> 1
    columns = []
    for row in (at, (at & -8) + 2 * step + ((at >> 2) & 1)):
        columns += [jnp.where(row < 256, row, -1), jnp.where(row < 256, -1, row - 256)]
    columns = jnp.concatenate(columns + [at & 3], axis=0).astype(f32).T
    lane_slot = (iota((2 * n, n), 1) >> 5).astype(f32).astype(bf16)
    lanes = [(iota((2 * n, n), 1) + n * k).astype(f32).astype(bf16) for k in range(2)]
    one, zero = jnp.ones((2 * n, n), bf16), jnp.zeros((2 * n, n), bf16)
    masses = ret_ref[:, 2 * SLOTS : 2 * SLOTS + 8, :].reshape(chips * 8, 128)
    copies = []

    def gather(t):
        def column(k):
            first = 8 * k + 2 * t
            both = [jnp.broadcast_to(columns[:, c : c + 1], (n, n)) for c in (first, first + 1)]
            return jnp.concatenate(both, axis=0).astype(bf16)

        def pick(k):
            return jnp.concatenate(
                [jnp.where(column(k + side) == lane, one, zero) for side in range(2) for lane in lanes], axis=1
            )

        rows = [ret_ref[:, k * SLOTS + 8 * t : k * SLOTS + 8 * t + 8, :].reshape(chips * 8, 128) for k in range(2)]
        values = dot(pick(0), jnp.concatenate(rows, axis=1))
        mass = dot(pick(2), masses).astype(bf16)
        return values, jnp.where(column(4) == lane_slot, mass, zero)

    def merge(t, values, wide):
        total, top = wide[:, :D], wide[:, D:]
        highest = jnp.maximum(top[:n], top[n:])
        w0 = jnp.exp2(top[:n] - highest)
        w1 = jnp.exp2(top[n:] - highest)
        merged = (w0 * values[:n] + w1 * values[n:]) / (w0 * total[:n] + w1 * total[n:])
        out_ref[t] = merged.astype(bf16)
        copies.append(pltpu.make_async_copy(out_ref.at[t], out_hbm.at[t], out_sem.at[t]))
        copies[-1].start()

    ahead = [gather(0)]
    for t in range(steps):
        if t + 1 < steps:
            ahead.append(gather(t + 1))
        values, mass = ahead[t]
        merge(t, values, dot(mass, widen))
    for copy in copies:
        copy.wait()


def near(x):
    return pltpu.with_memory_space_constraint(x, pltpu.VMEM)


def hbm(x):
    return pltpu.with_memory_space_constraint(x, pltpu.HBM)


def call(kernel, name, mib, outs, args, scratch=()):
    spec = pl.BlockSpec(memory_space=pltpu.VMEM)
    single = not isinstance(outs, tuple)
    return pl.pallas_call(
        kernel,
        out_shape=outs,
        in_specs=[spec] * len(args),
        out_specs=spec if single else tuple(spec for _ in outs),
        scratch_shapes=list(scratch),
        compiler_params=pltpu.CompilerParams(vmem_limit_bytes=mib << 20),
        name=name,
    )(*args)


def body(queries, probes, keys, values, bucket_home, bucket_rows):
    chips = lax.axis_size("y") * lax.axis_size("col")
    steps = queries.shape[0]
    swap = [(0, 1), (1, 0)]
    k_own, v_own = keys[0], values[0]
    k_other = lax.ppermute(k_own, "core", swap)
    v_other = lax.ppermute(v_own, "core", swap)
    home = bucket_home.reshape(1, 128)
    rows = bucket_rows.reshape(1, 128)
    far = pl.BlockSpec(memory_space=pltpu.HBM)
    send, pos = pl.pallas_call(
        dispatch_kernel,
        out_shape=(jax.ShapeDtypeStruct((chips, SLOTS, D), bf16), pltpu.VMEM((2 * steps, 128), f32)),
        in_specs=[far] * 3,
        out_specs=(far, pl.BlockSpec(memory_space=pltpu.VMEM)),
        scratch_shapes=[
            pltpu.VMEM((steps, 2, 128), i32),
            pltpu.VMEM((1, 128), i32),
            pltpu.VMEM(queries.shape, bf16),
            pltpu.VMEM((chips, SLOTS, D), bf16),
            pltpu.SemaphoreType.DMA((3,)),
            pltpu.SemaphoreType.DMA((steps,)),
        ],
        compiler_params=pltpu.CompilerParams(vmem_limit_bytes=16 << 20),
        name="dispatch",
    )(hbm(probes.transpose(0, 2, 1)), hbm(home), hbm(queries))
    recv = lax.all_to_all(send, ("y", "col"), split_axis=0, concat_axis=0, tiled=True)
    k, vt, valid, stat = call(
        prepare_kernel, "prepare", 16,
        (
            pltpu.VMEM((2, 4, KB, D), bf16),
            pltpu.VMEM((2, 4, D, KB), bf16),
            pltpu.VMEM((2, 4, 16, KB), bf16),
            pltpu.VMEM((2, 8, D), f32),
        ),
        (home, rows, hbm(k_own), hbm(v_own), k_other, v_other),
    )
    padded = chips * 16 + QB
    ret = call(
        attention_kernel, "attention", 24,
        pltpu.VMEM((chips, RET, 128), bf16),
        (home, rows, near(recv), near(k), near(vt), near(valid), near(stat)),
        (
            pltpu.VMEM((2, padded, D), bf16),
            pltpu.VMEM((2, padded, D + 128), bf16),
            pltpu.VMEM((D, QB), bf16),
            pltpu.VMEM(((H - EARLY) * HD, QB), bf16),
            pltpu.VMEM((H, KB, QB), bf16),
            pltpu.VMEM((H, HD + 16, QB), f32),
            pltpu.VMEM((H, 8, QB), f32),
        ),
    )
    back = lax.all_to_all(ret, ("y", "col"), split_axis=0, concat_axis=0, tiled=True)
    return pl.pallas_call(
        combine_kernel,
        out_shape=jax.ShapeDtypeStruct(queries.shape, bf16),
        in_specs=[pl.BlockSpec(memory_space=pltpu.VMEM)] * 2,
        out_specs=far,
        scratch_shapes=[pltpu.VMEM(queries.shape, bf16), pltpu.SemaphoreType.DMA((steps,))],
        compiler_params=pltpu.CompilerParams(vmem_limit_bytes=24 << 20),
        name="combine",
    )(near(pos), near(back))


def solution(mesh):
    rows, columns = mesh.devices.shape
    split = Mesh(mesh.devices.reshape(rows // 2, 2, columns), ("y", "core", "col"))
    every = ("y", "core", "col")
    return jax.shard_map(
        body,
        mesh=split,
        in_specs=(
            P(None, every, None),
            P(None, every, None),
            P(every, None, None),
            P(every, None, None),
            P(),
            P(),
        ),
        out_specs=P(None, every, None),
        check_vma=False,
    )
```

```python
import math

import jax
import jax.numpy as jnp
from jax import lax
from jax.experimental import pallas as pl
from jax.experimental.pallas import tpu as pltpu
from jax.sharding import Mesh, PartitionSpec as P

H = 8
HD = 32
D = 256
KB = 256
QB = 256
EARLY = 4
SLOTS = 32
RET = 72
SCALE2 = math.log2(math.e) / math.sqrt(HD)
TINY = 2.0**-60
SAFE = 80.0
NORMS = (SAFE / SCALE2) ** 2 / 1.05

f32 = jnp.float32
bf16 = jnp.bfloat16
i32 = jnp.int32


def iota(shape, dim):
    return lax.broadcasted_iota(i32, shape, dim)


def dot(a, b):
    return jnp.dot(a, b, preferred_element_type=f32)


def dot_t(a, b):
    return lax.dot_general(a, b, (((1,), (1,)), ((), ())), preferred_element_type=f32)


def ones_where(cond):
    return jnp.where(cond, 1.0, 0.0).astype(bf16)


def pick_rows(index, shape):
    along = 1 if index.shape[1] == 1 else 0
    grid = iota(shape, along).astype(f32).astype(bf16)
    return jnp.where(grid == index.astype(bf16), jnp.ones(shape, bf16), jnp.zeros(shape, bf16))


def dispatch_kernel(probes_hbm, home_hbm, q_hbm, send_hbm, pos_ref, probes_ref, home_ref, q_ref, send_ref, in_sem, out_sem):
    copies = [
        pltpu.make_async_copy(source, target, in_sem.at[k])
        for k, (source, target) in enumerate(((home_hbm, home_ref), (probes_hbm, probes_ref), (q_hbm, q_ref)))
    ]
    for copy in copies:
        copy.start()
    steps = probes_ref.shape[0]
    n = 128
    tri = jnp.concatenate(
        [ones_where(iota((n, n), 0) < iota((n, n), 1)), jnp.ones((n, n), bf16)], axis=1
    )
    eye = iota((n, n), 0) == iota((n, n), 1)
    bucket = iota((n, n), 0)
    copies[0].wait()
    home_row = jnp.broadcast_to(home_ref[...].astype(f32), (n, n))
    home = dot(jnp.where(eye, home_row, 0.0).astype(bf16), jnp.ones((n, n), bf16)).astype(i32)
    core = (home >> 4) & 1
    chip = ((home >> 5) << 4) + (home & 15)
    base = (chip * 8 + core * 4).astype(f32)
    copies[1].wait()
    hits = [[bucket == probes_ref[t, j : j + 1, :] for j in range(2)] for t in range(steps)]
    counts = [[dot(ones_where(hit), tri) for hit in pair] for pair in hits]
    pos_rows = []
    for t in range(steps):
        before = base
        for j in range(2):
            mine = jnp.where(hits[t][j], counts[t][j][:, :n] + before, 0.0)
            pos_rows.append(jnp.sum(mine, axis=0, keepdims=True))
            before = before + counts[t][j][:, n:]
    pos = jnp.concatenate(pos_rows, axis=0)
    pos_ref[...] = pos
    rows = 256
    chips = rows // 8
    copies[2].wait()
    out_copies = []
    for t in range(steps):
        lead = q_ref[t, :, :n]
        tiny = (iota((n, n), 1) == 0) & (jnp.abs(lead.astype(f32)) < TINY)
        queries = jnp.concatenate([jnp.where(tiny, jnp.full(lead.shape, TINY, bf16), lead), q_ref[t, :, n:]], axis=1)
        for block in range(send_ref.shape[0] // chips):
            pick = sum(pick_rows(pos[2 * t + j : 2 * t + j + 1] - block * rows, (rows, n)) for j in range(2))
            out = dot(pick, queries).astype(bf16)
            send_ref[block * chips : (block + 1) * chips, 8 * t : 8 * t + 8, :] = out.reshape(chips, 8, D)
            part = (pl.ds(block * chips, chips), pl.ds(8 * t, 8), slice(None))
            out_copies.append(pltpu.make_async_copy(send_ref.at[part], send_hbm.at[part], out_sem.at[t, block]))
            out_copies[-1].start()
    for copy in out_copies:
        copy.wait()


def bucket_sizes(home_ref, rows_ref):
    core = lax.axis_index("core")
    columns = lax.axis_size("col")
    device = (lax.axis_index("y") * 2 + core) * columns + lax.axis_index("col")
    partner = device + columns * (1 - 2 * core)
    rows = rows_ref[...].astype(f32)

    def size(where):
        return jnp.sum(jnp.where(home_ref[...] == where, rows, 0.0)).astype(i32)

    return core, size(device), size(partner)


def prepare_kernel(home_ref, rows_ref, k_own, v_own, k_other, v_other, k_ref, vt_ref, valid_ref, stat_ref):
    _, own, other = bucket_sizes(home_ref, rows_ref)
    head_sum = ones_where((iota((D, 128), 0) // HD) == iota((D, 128), 1))
    for u in range(2):
        key_ref = (k_own, k_other)[u]
        value_ref = (v_own, v_other)[u]
        count = (own, other)[u]
        norm = jnp.zeros((KB, 128), f32)
        for kb in range(1024 // KB):
            key = key_ref[kb * KB : (kb + 1) * KB, :]
            k_ref[u, kb] = key
            norm = jnp.maximum(norm, dot(key * key, head_sum))
            valid = ones_where((iota((16, KB), 1) + kb * KB) < count)
            valid_ref[u, kb] = valid
            value = value_ref[kb * KB : (kb + 1) * KB, :]
            vt_ref[u, kb] = value.T * valid[0:1, :]
        stat_ref[u] = jnp.full((8, D), jnp.max(norm), f32)


def attention_kernel(
    home_ref, rows_ref, recv_ref, k_ref, vt_ref, valid_ref, stat_ref, ret_ref,
    qc_ref, oc_ref, qt_ref, late_ref, p_ref, acc_ref, max_ref,
):
    n = 256
    half = n // 2
    srcs = n // SLOTS
    groups = recv_ref.shape[0] // srcs
    core, own, other = bucket_sizes(home_ref, rows_ref)

    def key_count(u):
        return jnp.where(u == 0, own, other)

    def slots(g):
        return recv_ref[srcs * g : srcs * (g + 1)].reshape(n, D)

    row = iota((groups, n), 0)
    side = (iota((1, n), 1) >> 2) & 1
    heads = ones_where((iota((16, D), 1) // HD) == iota((16, D), 0))
    norm = jnp.zeros((groups, n), f32)
    unsafe = jnp.zeros((8, n), f32)
    keys_norm = jnp.maximum(stat_ref[0, 0:1, :], stat_ref[1, 0:1, :])
    for g in range(groups):
        q = slots(g)
        squares = dot_t(heads, q * q)[0:8, :]
        unsafe = jnp.maximum(unsafe, jnp.where(squares * keys_norm <= NORMS, 0.0, 1.0))
        norm = jnp.where(row == g, jnp.sum(squares, axis=0, keepdims=True), norm)
    live = jnp.where(norm <= 0.0, 0.0, 1.0)
    side_in = (iota((n, n), 0) >> 2) & 1
    side_out = (iota((n, n), 1) >> 2) & 1
    upper = ones_where((iota((n, n), 0) < iota((n, n), 1)) & (side_in == side_out))
    rank = dot(live.astype(bf16), upper)
    code = jnp.where(live > 0.5, rank + (side * half).astype(f32), -1.0)
    code_t = code.T
    offsets = [[], []]
    ends = []
    for j in range(2):
        sizes = jnp.sum(jnp.where(side == j, live, 0.0), axis=1, keepdims=True).astype(i32)
        offset = jnp.int32(0)
        for g in range(groups):
            offsets[j].append(pl.multiple_of(offset, 16))
            offset = offset + ((sizes[g, 0] + 15) >> 4) * 16
        ends.append(offset)
    for g in range(groups):
        rows = dot(pick_rows(code[g : g + 1, :], (n, n)), slots(g)).astype(bf16)
        for j in range(2):
            qc_ref[j, pl.ds(offsets[j][g], half), :] = rows[j * half : (j + 1) * half]
    for j in range(2):
        after = pl.multiple_of(offsets[j][groups - 1] + half, 16)
        qc_ref[j, pl.ds(after, QB), :] = jnp.zeros((QB, D), bf16)
    fast = jnp.max(unsafe) < 0.5

    chunks = [(end + QB - 1) // QB for end in ends]
    blocks = [(key_count(j ^ core) + KB - 1) // KB for j in range(2)]

    def pick(j, pair):
        return jnp.where(j == 0, pair[0], pair[1])

    def queries_of(h):
        pieces = [
            qt_ref[h * HD : (h + 1) * HD, :] if k == h % 4 else jnp.zeros((HD, QB), bf16)
            for k in range(4)
        ]
        return jnp.concatenate(pieces, axis=0)

    def keys_of(u, kb, h):
        return k_ref[u, kb, :, (h // 4) * 128 : (h // 4 + 1) * 128]

    def finish(j, start, values, masses):
        count = values.shape[1]
        row = iota((8, count), 0)
        tiles = []
        for hh in range(4):
            low, high = masses(hh), masses(hh + 4)
            tile = jnp.zeros((8, count), f32)
            for k in range(len(low)):
                tile = jnp.where((row & 3) == k, jnp.where(row < 4, low[k], high[k]), tile)
            tiles.append(tile)
        wide = jnp.concatenate([values] + tiles * 4, axis=0).astype(bf16)
        oc_ref[j, pl.ds(start, count), :] = wide.T

    def two(total):
        high = total.astype(bf16).astype(f32)
        return high, total - high

    def weights(u, kb, h, queries):
        p_ref[h] = jnp.exp2(dot(keys_of(u, kb, h), queries) * SCALE2).astype(bf16)

    def late_queries_of(h):
        part = late_ref[(h - EARLY) * HD : (h - EARLY + 1) * HD, :]
        return jnp.concatenate([part if k == h % 4 else jnp.zeros((HD, QB), bf16) for k in range(4)], axis=0)

    def load_queries(j, ch):
        qt_ref[...] = qc_ref[j, pl.ds(pl.multiple_of(ch * QB, QB), QB), :].T

    def add_values(u, kb, h, keep):
        lhs = jnp.concatenate([vt_ref[u, kb, h * HD : (h + 1) * HD, :], valid_ref[u, kb]], axis=0)
        acc_ref[h] = acc_ref[h] * keep + dot(lhs, p_ref[h])

    def fast_item(index, carry):
        j, ch, kb = carry
        ends_chunk = kb + 1 == pick(j, blocks)
        kb_next = jnp.where(ends_chunk, 0, kb + 1)
        ch_next = jnp.where(ends_chunk, ch + 1, ch)
        ends_bucket = ch_next == pick(j, chunks)
        ch_next = jnp.where(ends_bucket, 0, ch_next)
        j_next = jnp.minimum(jnp.where(ends_bucket, j + 1, j), 1)

        @pl.when(kb == 0)
        def _():
            late_ref[...] = qt_ref[EARLY * HD :, :]

        @pl.when(ends_chunk)
        def _():
            load_queries(j_next, ch_next)

        u, u_next = j ^ core, j_next ^ core
        keep = jnp.where(kb == 0, 0.0, 1.0)
        for h in range(EARLY, H):
            weights(u, kb, h, late_queries_of(h))
        add_values(u, kb, 0, keep)
        add_values(u, kb, 1, keep)
        for h in range(EARLY):
            weights(u_next, kb_next, h, queries_of(h))
            if h + 2 < EARLY:
                add_values(u, kb, h + 2, keep)
        for h in range(EARLY, H):
            add_values(u, kb, h, keep)

        @pl.when(ends_chunk)
        def _():
            finish(
                j, pl.multiple_of(ch * QB, QB),
                jnp.concatenate([acc_ref[h, 0:HD, :] for h in range(H)], axis=0),
                lambda h: two(acc_ref[h, HD : HD + 8, :]),
            )

        return j_next, ch_next, kb_next

    def slow_chunk(j, u, start, blocks, keys):
        acc_ref[...] = jnp.zeros(acc_ref.shape, f32)
        max_ref[...] = jnp.full(max_ref.shape, -3e38, f32)
        qt_ref[...] = qc_ref[j, pl.ds(start, QB), :].T

        def scores(kb, h):
            s = dot(keys_of(u, kb, h), queries_of(h)) * SCALE2
            return s, (iota((KB, QB), 0) + kb * KB) < keys

        def find(kb, carry):
            for h in range(H):
                s, valid = scores(kb, h)
                top = jnp.max(jnp.where(valid, s, -3e38), axis=0, keepdims=True)
                max_ref[h] = jnp.maximum(max_ref[h], top)
            return carry

        def block(kb, carry):
            for h in range(H):
                s, valid = scores(kb, h)
                p = jnp.where(valid, jnp.exp2(s - max_ref[h, 0:1, :]), 0.0).astype(bf16)
                lhs = jnp.concatenate([vt_ref[u, kb, h * HD : (h + 1) * HD, :], valid_ref[u, kb]], axis=0)
                acc_ref[h] += dot(lhs, p)
            return carry

        lax.fori_loop(0, blocks, find, 0)
        lax.fori_loop(0, blocks, block, 0)

        def masses(h):
            mass = jnp.log2(acc_ref[h, HD : HD + 8, :]) + max_ref[h]
            top, rest = two(mass)
            rest = rest.astype(bf16).astype(f32)
            return two(jnp.exp2(mass - top - rest)) + (top, rest)

        values = [acc_ref[h, 0:HD, :] / acc_ref[h, HD : HD + 1, :] for h in range(H)]
        finish(j, start, jnp.concatenate(values, axis=0), masses)

    @pl.when(fast)
    def _():
        start = jnp.where(chunks[0] > 0, 0, 1)
        load_queries(start, 0)
        acc_ref[...] = jnp.zeros(acc_ref.shape, f32)
        for h in range(EARLY):
            weights(start ^ core, 0, h, queries_of(h))
        total = chunks[0] * blocks[0] + chunks[1] * blocks[1]
        lax.fori_loop(0, total, fast_item, (start, jnp.int32(0), jnp.int32(0)))

    @pl.when(jnp.logical_not(fast))
    def _():
        def bucket(j, carry):
            def chunk(ch, carry):
                slow_chunk(j, j ^ core, pl.multiple_of(ch * QB, QB), pick(j, blocks), key_count(j ^ core))
                return carry

            return lax.fori_loop(0, pick(j, chunks), chunk, carry)

        lax.fori_loop(0, 2, bucket, 0)

    for j in range(2):
        done = pl.multiple_of(chunks[j] * QB, QB)
        oc_ref[j, pl.ds(done, half), :] = jnp.zeros((half, D + 128), bf16)

    own_lanes = (iota((8, 128), 1) >> 5) == (iota((8, 128), 0) & 3)
    own_lanes = jnp.concatenate([jnp.where(own_lanes, 1.0, 0.0)] * (n // 8), axis=0)
    mass_row = iota((8 * srcs, n), 0)
    mass_slot = iota((8 * srcs, n), 1)
    collect = ones_where(mass_row == (mass_slot >> 5) * 8 + ((mass_slot & 31) >> 2))

    def unpack(g):
        scatter = pick_rows(code_t[:, g : g + 1], (n, n))
        packed = jnp.concatenate([oc_ref[j, pl.ds(offsets[j][g], half), :] for j in range(2)], axis=0)
        return dot(scatter, packed)

    def write(g, rows):
        for k in range(2):
            out = rows[:, k * 128 : (k + 1) * 128].astype(bf16)
            ret_ref[srcs * g : srcs * (g + 1), k * SLOTS : (k + 1) * SLOTS, :] = out.reshape(srcs, SLOTS, 128)
        return (rows[:, D:] * own_lanes).astype(bf16)

    ahead = [unpack(g) for g in range(2)]
    spread = []
    for g in range(groups):
        if g + 2 < groups:
            ahead.append(unpack(g + 2))
        spread.append(write(g, ahead[g]))
    for g in range(groups):
        out = dot(collect, spread[g]).astype(bf16)
        ret_ref[srcs * g : srcs * (g + 1), 2 * SLOTS : 2 * SLOTS + 8, :] = out.reshape(srcs, 8, 128)


def combine_kernel(pos_ref, ret_ref, out_hbm, out_ref, out_sem):
    n = 128
    steps = out_ref.shape[0]
    chips = ret_ref.shape[0]
    lane_in = iota((n, D), 0) & 31
    head = iota((n, D), 1) // HD
    same_head = (lane_in >> 2) == 2 * (head & 3) + (head >> 2)
    widen = jnp.concatenate(
        [ones_where(same_head & ((lane_in & 3) < 2)), ones_where(same_head & ((lane_in & 3) >= 2))], axis=1
    )
    at = pos_ref[...].astype(i32)
    step = iota(at.shape, 0) >> 1
    columns = []
    for row in (at, (at & -8) + 2 * step + ((at >> 2) & 1)):
        columns += [jnp.where(row < 256, row, -1), jnp.where(row < 256, -1, row - 256)]
    columns = jnp.concatenate(columns + [at & 3], axis=0).astype(f32).T
    lane_slot = (iota((2 * n, n), 1) >> 5).astype(f32).astype(bf16)
    lanes = [(iota((2 * n, n), 1) + n * k).astype(f32).astype(bf16) for k in range(2)]
    one, zero = jnp.ones((2 * n, n), bf16), jnp.zeros((2 * n, n), bf16)
    masses = ret_ref[:, 2 * SLOTS : 2 * SLOTS + 8, :].reshape(chips * 8, 128)
    copies = []

    def gather(t):
        def column(k):
            first = 8 * k + 2 * t
            both = [jnp.broadcast_to(columns[:, c : c + 1], (n, n)) for c in (first, first + 1)]
            return jnp.concatenate(both, axis=0).astype(bf16)

        def pick(k):
            return jnp.concatenate(
                [jnp.where(column(k + side) == lane, one, zero) for side in range(2) for lane in lanes], axis=1
            )

        rows = [ret_ref[:, k * SLOTS + 8 * t : k * SLOTS + 8 * t + 8, :].reshape(chips * 8, 128) for k in range(2)]
        values = dot(pick(0), jnp.concatenate(rows, axis=1))
        mass = dot(pick(2), masses).astype(bf16)
        return values, jnp.where(column(4) == lane_slot, mass, zero)

    def merge(t, values, wide):
        total, top = wide[:, :D], wide[:, D:]
        highest = jnp.maximum(top[:n], top[n:])
        w0 = jnp.exp2(top[:n] - highest)
        w1 = jnp.exp2(top[n:] - highest)
        merged = (w0 * values[:n] + w1 * values[n:]) / (w0 * total[:n] + w1 * total[n:])
        out_ref[t] = merged.astype(bf16)
        copies.append(pltpu.make_async_copy(out_ref.at[t], out_hbm.at[t], out_sem.at[t]))
        copies[-1].start()

    ahead = [gather(0)]
    for t in range(steps):
        if t + 1 < steps:
            ahead.append(gather(t + 1))
        values, mass = ahead[t]
        merge(t, values, dot(mass, widen))
    for copy in copies:
        copy.wait()


def near(x):
    return pltpu.with_memory_space_constraint(x, pltpu.VMEM)


def hbm(x):
    return pltpu.with_memory_space_constraint(x, pltpu.HBM)


def call(kernel, name, mib, outs, args, scratch=()):
    spec = pl.BlockSpec(memory_space=pltpu.VMEM)
    single = not isinstance(outs, tuple)
    return pl.pallas_call(
        kernel,
        out_shape=outs,
        in_specs=[spec] * len(args),
        out_specs=spec if single else tuple(spec for _ in outs),
        scratch_shapes=list(scratch),
        compiler_params=pltpu.CompilerParams(vmem_limit_bytes=mib << 20),
        name=name,
    )(*args)


def body(queries, probes, keys, values, bucket_home, bucket_rows):
    chips = lax.axis_size("y") * lax.axis_size("col")
    steps = queries.shape[0]
    swap = [(0, 1), (1, 0)]
    k_own, v_own = keys[0], values[0]
    k_other = lax.ppermute(k_own, "core", swap)
    v_other = lax.ppermute(v_own, "core", swap)
    home = bucket_home.reshape(1, 128)
    rows = bucket_rows.reshape(1, 128)
    far = pl.BlockSpec(memory_space=pltpu.HBM)
    send, pos = pl.pallas_call(
        dispatch_kernel,
        out_shape=(jax.ShapeDtypeStruct((chips, SLOTS, D), bf16), pltpu.VMEM((2 * steps, 128), f32)),
        in_specs=[far] * 3,
        out_specs=(far, pl.BlockSpec(memory_space=pltpu.VMEM)),
        scratch_shapes=[
            pltpu.VMEM((steps, 2, 128), i32),
            pltpu.VMEM((1, 128), i32),
            pltpu.VMEM(queries.shape, bf16),
            pltpu.VMEM((chips, SLOTS, D), bf16),
            pltpu.SemaphoreType.DMA((3,)),
            pltpu.SemaphoreType.DMA((steps, chips * 8 // 256)),
        ],
        compiler_params=pltpu.CompilerParams(vmem_limit_bytes=16 << 20),
        name="dispatch",
    )(hbm(probes.transpose(0, 2, 1)), hbm(home), hbm(queries))
    recv = lax.all_to_all(send, ("y", "col"), split_axis=0, concat_axis=0, tiled=True)
    k, vt, valid, stat = call(
        prepare_kernel, "prepare", 16,
        (
            pltpu.VMEM((2, 4, KB, D), bf16),
            pltpu.VMEM((2, 4, D, KB), bf16),
            pltpu.VMEM((2, 4, 16, KB), bf16),
            pltpu.VMEM((2, 8, D), f32),
        ),
        (home, rows, hbm(k_own), hbm(v_own), k_other, v_other),
    )
    padded = chips * 16 + QB
    ret = call(
        attention_kernel, "attention", 24,
        pltpu.VMEM((chips, RET, 128), bf16),
        (home, rows, near(recv), near(k), near(vt), near(valid), near(stat)),
        (
            pltpu.VMEM((2, padded, D), bf16),
            pltpu.VMEM((2, padded, D + 128), bf16),
            pltpu.VMEM((D, QB), bf16),
            pltpu.VMEM(((H - EARLY) * HD, QB), bf16),
            pltpu.VMEM((H, KB, QB), bf16),
            pltpu.VMEM((H, HD + 16, QB), f32),
            pltpu.VMEM((H, 8, QB), f32),
        ),
    )
    back = lax.all_to_all(ret, ("y", "col"), split_axis=0, concat_axis=0, tiled=True)
    return pl.pallas_call(
        combine_kernel,
        out_shape=jax.ShapeDtypeStruct(queries.shape, bf16),
        in_specs=[pl.BlockSpec(memory_space=pltpu.VMEM)] * 2,
        out_specs=far,
        scratch_shapes=[pltpu.VMEM(queries.shape, bf16), pltpu.SemaphoreType.DMA((steps,))],
        compiler_params=pltpu.CompilerParams(vmem_limit_bytes=24 << 20),
        name="combine",
    )(near(pos), near(back))


def solution(mesh):
    rows, columns = mesh.devices.shape
    split = Mesh(mesh.devices.reshape(rows // 2, 2, columns), ("y", "core", "col"))
    every = ("y", "core", "col")
    return jax.shard_map(
        body,
        mesh=split,
        in_specs=(
            P(None, every, None),
            P(None, every, None),
            P(every, None, None),
            P(every, None, None),
            P(),
            P(),
        ),
        out_specs=P(None, every, None),
        check_vma=False,
    )
```
